32 devices in a mesh: ens: 8 (over z, x), row: 2 (over y), col: 2 (over core).
Axes of the slice: x: 2, y: 2, z: 4, core: 2. Of those that a mesh axis runs over, the one named last changes fastest.
Arguments:
- states: float32 [16, 16, 4096], P('ens', None, ('row', 'col')), parts along dimension 0, may hold values from -4 to 4
- jacobian: bfloat16 [32768, 4096], P(('ens', 'row'), 'col'), parts along dimension 0, as said below
- step_sizes: float32 [16, 1], P('ens'), parts along dimension 0, may hold values from 0.75 to 1.5
Outputs:
- new_states: float32 [16, 16, 4096], P('ens', None, ('row', 'col')), parts along dimension 0
The draws below stay inside these ranges and needn't reach their ends.
There are 8 independent parts, one for each index of `ens`. The reference program is written for one: setup_inputs(seed, part) draws one part's arguments, and reference() takes and returns one part's arrays. A program takes and returns all parts, laid end to end along the dimension named above; each array names one. Nothing has to cross between parts.
Inputs may be any that keep to these rules, and one draw needn't show every extreme that they name: `jacobian`: the diagonal lies between -40 and -1 apart from a term as small as the others, whose magnitude is at most 24 / sqrt(4096).
All inputs are finite; a program needn't handle non-finite values.
Results may differ from the reference program's by a relative error of at most 0.0083.
Values may be sent and summed in bfloat16 or wider, within the bound.
A program may use at most 64 MiB of HBM per device.

```python
import math
import jax
import jax.numpy as jnp
from jax import lax

N = 4096
COLS = 16
BLOCKS = 12
STEPS = 1
BATCH = 2


def draw_jacobian(key, part):
    first_key, second_key = jax.random.split(jax.random.fold_in(key, 11))
    spread = 4.0 / math.sqrt(N)
    rough = jnp.clip(jax.random.normal(first_key, (N, N), jnp.float32), -6.0, 6.0) * spread
    rates = jnp.exp(jax.random.uniform(second_key, (N,), jnp.float32, 0.0, math.log(40.0)))
    return (rough - jnp.diag(rates)).astype(jnp.bfloat16)


def block_scale(key, shape, pieces, low, top_value):
    loudness = 1.0
    for axis_at, parts in pieces:
        steps = jax.random.uniform(jax.random.fold_in(jax.random.fold_in(key, 6), axis_at), (parts,), jnp.float32, low / len(pieces), top_value / len(pieces))
        loudness = loudness * jnp.repeat(jnp.exp(steps), shape[axis_at] // parts).reshape((-1,) + (1,) * (len(shape) - 1 - axis_at))
    return loudness


def gaussian(stream_key, shape, scale, reach, shards=(), held_as=jnp.bfloat16):
    array = scale * jax.random.normal(stream_key, shape, jnp.float32)
    if shards:
        array = array * block_scale(stream_key, shape, shards, -0.22, 0.18)
    return jnp.clip(array, -reach, reach).astype(held_as)


def setup_inputs(seed: int = 0, part: int = 0) -> dict:
    keys = jax.random.split(jax.random.key(seed), 4)
    part_keys = jax.random.split(jax.random.fold_in(keys[3], part), 4)
    return {
        "states": gaussian(part_keys[0], (BATCH, COLS, N), 1.0, 4.0, ((2, 4),), jnp.float32),
        "jacobian": draw_jacobian(jax.random.fold_in(jax.random.fold_in(keys[3], part), 71), part),
        "step_sizes": jnp.clip(jnp.exp(jax.random.uniform(part_keys[2], (BATCH, STEPS), jnp.float32, math.log(0.75), math.log(1.5))), 0.75, 1.5),
    }


precise = lax.Precision.HIGHEST
squarings = 10
taylor_degree = 8

def exponential(matrix):
    scaled = matrix / 2.0 ** squarings
    identity = jnp.eye(matrix.shape[-1], dtype=jnp.float32)
    result = jnp.broadcast_to(identity, matrix.shape)
    for degree in range(taylor_degree, 0, -1):
        result = identity + jnp.matmul(scaled, result, precision=precise) / degree
    for squaring in range(squarings):
        result = jnp.matmul(result, result, precision=precise)
    return result

def apply_full(vectors, matrix):
    rounded = lax.optimization_barrier(vectors.astype(jnp.bfloat16)).astype(jnp.float32)
    return jnp.einsum('bcm,nm->bcn', rounded, matrix, precision=precise)

def reference(states, jacobian, step_sizes):
    matrix = jacobian.astype(jnp.float32)
    members = states.shape[0]
    columns = states.shape[1]
    length = states.shape[2]
    krylov = BLOCKS * columns
    for step_index in range(STEPS):
        forcing = apply_full(states, matrix) - states * states * states / 3.0
        root_gram = jnp.einsum('bpn,bqn->bpq', forcing, forcing, precision=precise)
        root_lower = jnp.linalg.cholesky(root_gram)
        leading = lax.linalg.triangular_solve(root_lower, forcing, left_side=True, lower=True)
        krylov_basis = jnp.zeros((members, krylov, length), jnp.float32).at[:, :columns].set(leading)
        hessenberg = jnp.zeros((members, krylov, krylov), jnp.float32)
        for block_index in range(BLOCKS):
            start = block_index * columns
            current = krylov_basis[:, start:start + columns]
            images = apply_full(current, matrix)
            projection = jnp.einsum('bkn,bqn->bkq', krylov_basis, images, precision=precise)
            hessenberg = hessenberg.at[:, :, start:start + columns].set(projection)
            if block_index + 1 < BLOCKS:
                reduced = images - jnp.einsum('bkq,bkn->bqn', projection, krylov_basis, precision=precise)
                gram_matrix = jnp.einsum('bpn,bqn->bpq', reduced, reduced, precision=precise)
                lower_factor = jnp.linalg.cholesky(gram_matrix)
                next_block = lax.linalg.triangular_solve(lower_factor, reduced, left_side=True, lower=True)
                hessenberg = hessenberg.at[:, start + columns:start + 2 * columns, start:start + columns].set(jnp.swapaxes(lower_factor, 1, 2))
                krylov_basis = krylov_basis.at[:, start + columns:start + 2 * columns].set(next_block)
        step_size = step_sizes[:, step_index][:, None, None]
        augmented = jnp.zeros((members, krylov + columns, krylov + columns), jnp.float32)
        augmented = augmented.at[:, :krylov, :krylov].set(step_size * hessenberg)
        augmented = augmented.at[:, :columns, krylov:].set(step_size * jnp.swapaxes(root_lower, 1, 2))
        exponent = exponential(augmented)
        phi_block = exponent[:, :krylov, krylov:]
        states = states + jnp.einsum('bkq,bkn->bqn', phi_block, krylov_basis, precision=precise)
    return states
```

```python
import functools

import jax
import jax.numpy as jnp
from jax import lax
from jax.experimental import pallas as pl
from jax.experimental.pallas import tpu as pltpu
from jax.sharding import PartitionSpec as P

BLOCKS = 12
SQUARINGS = 10
CHUNKS = 4
TILE = 512
GROUP = 16
LANES = 128
MESH = pl.DeviceIdType.MESH
NN = (((1,), (0,)), ((), ()))
NT = (((1,), (1,)), ((), ()))
f32, bf16 = jnp.float32, jnp.bfloat16


def split(value):
    high = value.astype(bf16)
    return high, (value - high.astype(f32)).astype(bf16)


def product(left, right, dims):
    rows = left[0].shape[0]
    both = jnp.concatenate(left, axis=0)
    wide = lax.dot_general(both, right[0], dims, preferred_element_type=f32)
    low = lax.dot_general(left[0], right[1], dims, preferred_element_type=f32)
    return wide[:rows] + (wide[rows:] + low)


def factor(gram, offset):
    columns = gram.shape[0]
    lanes_inv = lax.broadcasted_iota(jnp.int32, (columns, columns), 1)
    sub_inv = lax.broadcasted_iota(jnp.int32, (columns, columns), 0)
    inverse = jnp.where(lanes_inv == sub_inv, 1.0, 0.0).astype(f32)
    lanes = lax.broadcasted_iota(jnp.int32, (columns, offset[1]), 1)
    lower = jnp.zeros((columns, offset[1]), f32)
    sub = lax.broadcasted_iota(jnp.int32, (columns, LANES), 0)
    for base in range(0, columns, GROUP):
        held = [
            jnp.broadcast_to(gram[:, base + i : base + i + 1], (columns, LANES))
            for i in range(GROUP)
        ]
        for i in range(GROUP):
            k = base + i
            pivot = held[i][k : k + 1, :]
            root = lax.rsqrt(pivot)
            root = root * (1.5 - 0.5 * pivot * root * root)
            column = jnp.where(sub >= k, held[i] * root, 0.0)
            below = jnp.where(sub > k, column, 0.0)
            for later in range(i + 1, GROUP):
                index = base + later
                held[later] = held[later] - below * column[index : index + 1, :]
            wide = jnp.concatenate([column] * (offset[1] // LANES), axis=1)
            lower = jnp.where(lanes == offset[0] + k, wide, lower)
            row = gram[k : k + 1, :] * root[:, :columns]
            row_inv = inverse[k : k + 1, :] * root[:, :columns]
            gram = gram - below[:, :columns] * row
            inverse = jnp.where(sub_inv == k, row_inv, inverse - below[:, :columns] * row_inv)
    return inverse, lower


def kernel(
    nr, nc, states_ref, jac_hbm, steps_ref, out_ref,
    jac, first, own, gathered, acc, part_send, part_recv, vh, vl, zh, zl, cur, shift, state,
    result, result_recv, sums_send, sums_recv, aug,
    jac_sem, g_send, g_recv, p_send, p_recv, s_send, s_recv, x_send, x_recv, o_send, o_recv,
):
    members, columns, length = states_ref.shape
    cells = nc * length
    chunk = cells // CHUNKS
    share = CHUNKS // nc
    width = vh.shape[0]
    r, c = lax.axis_index("row"), lax.axis_index("col")
    other, beyond = 1 - c, 1 - r
    me = r * nc + c
    count = nr * nc
    home = c == r

    load = pltpu.make_async_copy(jac_hbm, jac, jac_sem)
    load.start()
    barrier = pltpu.get_barrier_semaphore()
    for step in range(1, count):
        peer = lax.rem(me + step, count)
        pl.semaphore_signal(
            barrier, inc=1, device_id={"row": peer // nc, "col": lax.rem(peer, nc)},
            device_id_type=MESH,
        )
    for b in range(members):
        rounded = states_ref[b].astype(bf16)
        for k in range(share):
            first[b, k] = rounded[:, k * chunk : (k + 1) * chunk]
    pl.semaphore_wait(barrier, count - 1)

    def remote(src, dst, send, recv, row, col):
        return pltpu.make_async_remote_copy(
            src_ref=src, dst_ref=dst, send_sem=send, recv_sem=recv,
            device_id={"row": row, "col": col}, device_id_type=MESH,
        )

    def opening(row, b, k):
        at = c * share + k
        return remote(
            first.at[b, k], gathered.at[0, b, at, :columns], g_send.at[row, b, at],
            g_recv.at[0, b, at], row, r,
        )

    def opened(b, at):
        return remote(
            first.at[0, 0], gathered.at[0, b, at, :columns], g_send.at[0, b, at],
            g_recv.at[0, b, at], c, other,
        )

    def block(slot, row, k):
        return remote(
            own.at[k], gathered.at[slot, c, k], g_send.at[row, 0, k], g_recv.at[slot, c, k],
            row, r,
        )

    def arrived(slot, b, k):
        return remote(
            own.at[k], gathered.at[slot, b, k], g_send.at[0, 0, k], g_recv.at[slot, b, k], c, other
        )

    def partial(slot):
        return remote(part_send, part_recv.at[slot], p_send, p_recv.at[slot], r, other)

    def sums(slot):
        return remote(sums_send, sums_recv.at[slot], s_send, s_recv.at[slot], beyond, c)

    swap = remote(states_ref.at[other], state.at[c], x_send, x_recv, r, other)

    for b in range(members):
        for k in range(share):
            opening(beyond, b, k).start()
    for b in range(members):
        for k in range(share):
            @pl.when(jnp.logical_not(home))
            def _():
                opening(r, b, k).start()

            @pl.when(home)
            def _():
                gathered[0, b, c * share + k, :columns] = first[b, k]
    swap.start()
    state[c] = states_ref[c]
    for ref in (vh, vl, zh, zl, aug, sums_send):
        ref[...] = jnp.zeros_like(ref)

    def exchange(slot):
        part_send[...] = acc[other, :columns] + acc[other, columns:]
        partial(slot).start()

    def finish(slot):
        return acc[c, :columns] + acc[c, columns:] + part_recv[slot]

    def place(now, slot):
        pair = split(now)
        cur[slot] = now
        vh[:columns], vl[:columns] = pair
        both = jnp.concatenate(pair, axis=0)
        for k in range(CHUNKS):
            own[k] = both[:, k * chunk : (k + 1) * chunk]
        return pair

    def send(slot):
        for k in range(CHUNKS):
            block(slot, beyond, k).start()

        @pl.when(jnp.logical_not(home))
        def _():
            for k in range(CHUNKS):
                block(slot, r, k).start()

        @pl.when(home)
        def _():
            for k in range(CHUNKS):
                gathered[slot, c, k] = own[k]

    def project(i):
        at = slice(i * LANES, (i + 1) * LANES)
        pair = vh[:columns], vl[:columns]
        sums_send[:, at] = product(pair, (vh[at], vl[at]), NT)

    load.wait()
    for k in range(CHUNKS):
        for b in range(members):
            @pl.when(jnp.logical_not(jnp.logical_and(home, k // share == c)))
            def _():
                opened(b, k).wait_recv()

        left = gathered[0, :, k, :columns].reshape(members * columns, chunk)
        for n in range(0, cells, TILE):
            term = lax.dot_general(
                left, jac[n : n + TILE, k * chunk : (k + 1) * chunk], NT,
                preferred_element_type=f32,
            ).reshape(members, columns, TILE)
            if k:
                term = term + acc[:, :columns, n : n + TILE]
            acc[:, :columns, n : n + TILE] = term
    part_send[...] = acc[other, :columns]
    partial(0).start()
    swap.wait()
    for b in range(members):
        for k in range(share):
            opening(beyond, b, k).wait_send()

            @pl.when(jnp.logical_not(home))
            def _():
                opening(r, b, k).wait_send()
    held = jnp.concatenate([state[h] for h in range(nc)], axis=1)
    cube = held * held * held / 3.0
    partial(0).wait()
    place(acc[c, :columns] + part_recv[0] - cube, 0)
    send(1)
    project(0)
    sums(0).start()

    def gather_sums(slot):
        sums(slot).wait()
        total = sums_send[...] + sums_recv[slot]
        lanes = lax.broadcasted_iota(jnp.int32, (columns, width), 1)
        return total, jnp.where(lanes >= columns, total, 0.0)

    def turn(t, carry):
        slot, before = lax.rem(t, 2), lax.rem(t + 1, 2)
        for k in range(CHUNKS):
            for b in range(members):
                @pl.when(jnp.logical_not(jnp.logical_and(home, b == c)))
                def _():
                    arrived(slot, b, k).wait_recv()

            left = gathered[slot, :, k].reshape(members * 2 * columns, chunk)
            for n in range(0, cells, TILE):
                term = lax.dot_general(
                    left, jac[n : n + TILE, k * chunk : (k + 1) * chunk], NT,
                    preferred_element_type=f32,
                ).reshape(members, 2 * columns, TILE)
                if k:
                    term = term + acc[:, :, n : n + TILE]
                acc[:, :, n : n + TILE] = term
        exchange(slot)
        total, projection = gather_sums(before)
        coefficients = split(projection)
        gram = total[:, :columns] - product(coefficients, coefficients, NT)
        inverse, lower = factor(gram, (t * columns, width))
        start = pl.multiple_of((t - 1) * columns, columns)
        aug[pl.ds(start, columns), :] = projection + lower
        inverse = split(inverse)
        shift[...] = product(coefficients, (zh[...], zl[...]), NN)
        for k in range(CHUNKS):
            block(slot, beyond, k).wait_send()

        @pl.when(jnp.logical_not(home))
        def _():
            for k in range(CHUNKS):
                block(slot, r, k).wait_send()

        partial(slot).wait()
        pair = place(product(inverse, split(finish(slot) - shift[...]), NN), slot)
        pl.when(t < BLOCKS)(lambda: send(before))
        here = pl.multiple_of(t * columns, columns)
        zh[pl.ds(here, columns), :], zl[pl.ds(here, columns), :] = pair
        reduced = cur[before] - product(coefficients, (vh[...], vl[...]), NN)
        new = split(product(inverse, split(reduced), NN))
        vh[pl.ds(here, columns), :], vl[pl.ds(here, columns), :] = new
        project(0)
        for i in range(1, width // LANES):
            pl.when((t + 1) * columns > i * LANES)(functools.partial(project, i))
        sums(slot).start()
        return carry

    lax.fori_loop(1, BLOCKS + 1, turn, 0)

    _, projection = gather_sums(BLOCKS % 2)
    aug[BLOCKS * columns : (BLOCKS + 1) * columns] = projection
    x = aug[...] * (steps_ref[c, 0] / 2.0**SQUARINGS)
    xs = split(x)
    x2 = product(xs, xs, NN)
    x2s = split(x2)
    x3 = product(xs, x2s, NN)
    x4 = product(x2s, x2s, NN)
    tail = x / 120.0 + x2 / 720.0 + x3 / 5040.0 + x4 / 40320.0
    aug[...] = x + x2 / 2.0 + x3 / 6.0 + x4 / 24.0 + product(split(x4), split(tail), NN)

    def square(index, carry):
        now = aug[...]
        pair = split(now)
        aug[...] = 2.0 * now + product(pair, pair, NN)
        return carry

    lax.fori_loop(0, SQUARINGS - 1, square, 0)
    now = aug[...]
    top = now[:columns]
    phi = split(2.0 * top + product(split(top), split(now), NN))
    for h in range(nc):
        at = slice(h * length, (h + 1) * length)
        result[h] = product(phi, (vh[:, at], vl[:, at]), NN)
    swap_out = remote(result.at[other], result_recv, o_send, o_recv, r, other)
    swap_out.start()
    out_ref[c] = states_ref[c] + result[c]
    swap_out.wait()
    out_ref[other] = states_ref[other] + result_recv[...]


def local(nr, nc, states, jacobian, step_sizes):
    members, columns, length = states.shape
    assert nr == nc == members == 2
    cells = nc * length
    chunk = cells // CHUNKS
    width = -(-(BLOCKS + 1) * columns // LANES) * LANES
    vmem = pl.BlockSpec(memory_space=pltpu.VMEM)
    dma = pltpu.SemaphoreType.DMA
    return pl.pallas_call(
        functools.partial(kernel, nr, nc),
        out_shape=jax.ShapeDtypeStruct(states.shape, f32),
        in_specs=[vmem, pl.BlockSpec(memory_space=pl.ANY), pl.BlockSpec(memory_space=pltpu.SMEM)],
        out_specs=vmem,
        scratch_shapes=[
            pltpu.VMEM(jacobian.shape, bf16),
            pltpu.VMEM((members, CHUNKS // nc, columns, chunk), bf16),
            pltpu.VMEM((CHUNKS, 2 * columns, chunk), bf16),
            pltpu.VMEM((2, members, CHUNKS, 2 * columns, chunk), bf16),
            pltpu.VMEM((members, 2 * columns, cells), f32),
            pltpu.VMEM((columns, cells), f32),
            pltpu.VMEM((2, columns, cells), f32),
            pltpu.VMEM((width, cells), bf16),
            pltpu.VMEM((width, cells), bf16),
            pltpu.VMEM((width, cells), bf16),
            pltpu.VMEM((width, cells), bf16),
            pltpu.VMEM((2, columns, cells), f32),
            pltpu.VMEM((columns, cells), f32),
            pltpu.VMEM((nc, columns, length), f32),
            pltpu.VMEM((nc, columns, length), f32),
            pltpu.VMEM((columns, length), f32),
            pltpu.VMEM((columns, width), f32),
            pltpu.VMEM((2, columns, width), f32),
            pltpu.VMEM((width, width), f32),
            dma, dma((nr, members, CHUNKS)), dma((2, members, CHUNKS)), dma, dma((2,)),
            dma, dma((2,)), dma, dma, dma, dma,
        ],
        compiler_params=pltpu.CompilerParams(
            collective_id=0, has_side_effects=True, vmem_limit_bytes=48 * 2**20
        ),
    )(states, jacobian, step_sizes)


def solution(mesh):
    placed = (P("ens", None, ("row", "col")), P(("ens", "row"), "col"), P("ens", None))
    return jax.shard_map(
        functools.partial(local, mesh.shape["row"], mesh.shape["col"]), mesh=mesh,
        in_specs=placed, out_specs=P("ens", None, ("row", "col")), check_vma=False,
    )
```

```python
import functools

import jax
import jax.numpy as jnp
from jax import lax
from jax.experimental import pallas as pl
from jax.experimental.pallas import tpu as pltpu
from jax.sharding import PartitionSpec as P

BLOCKS = 12
SQUARINGS = 10
CHUNKS = 4
TILE = 512
SIDE = 256
LOADS = 4
GROUP = 16
LANES = 128
MESH = pl.DeviceIdType.MESH
NN = (((1,), (0,)), ((), ()))
NT = (((1,), (1,)), ((), ()))
f32, bf16 = jnp.float32, jnp.bfloat16


def split(value):
    high = value.astype(bf16)
    return high, (value - high.astype(f32)).astype(bf16)


def product(left, right, dims):
    rows = left[0].shape[0]
    both = jnp.concatenate(left, axis=0)
    wide = lax.dot_general(both, right[0], dims, preferred_element_type=f32)
    low = lax.dot_general(left[0], right[1], dims, preferred_element_type=f32)
    return wide[:rows] + (wide[rows:] + low)


def factor(gram, offset):
    columns = gram.shape[0]
    lanes_inv = lax.broadcasted_iota(jnp.int32, (columns, columns), 1)
    sub_inv = lax.broadcasted_iota(jnp.int32, (columns, columns), 0)
    inverse = jnp.where(lanes_inv == sub_inv, 1.0, 0.0).astype(f32)
    lanes = lax.broadcasted_iota(jnp.int32, (columns, offset[1]), 1)
    lower = jnp.zeros((columns, offset[1]), f32)
    sub = lax.broadcasted_iota(jnp.int32, (columns, LANES), 0)
    for base in range(0, columns, GROUP):
        held = [
            jnp.broadcast_to(gram[:, base + i : base + i + 1], (columns, LANES))
            for i in range(GROUP)
        ]
        for i in range(GROUP):
            k = base + i
            pivot = held[i][k : k + 1, :]
            root = lax.rsqrt(pivot)
            root = root * (1.5 - 0.5 * pivot * root * root)
            column = jnp.where(sub >= k, held[i] * root, 0.0)
            below = jnp.where(sub > k, column, 0.0)
            for later in range(i + 1, GROUP):
                index = base + later
                held[later] = held[later] - below * column[index : index + 1, :]
            wide = jnp.concatenate([column] * (offset[1] // LANES), axis=1)
            lower = jnp.where(lanes == offset[0] + k, wide, lower)
            row = gram[k : k + 1, :] * root[:, :columns]
            row_inv = inverse[k : k + 1, :] * root[:, :columns]
            gram = gram - below[:, :columns] * row
            inverse = jnp.where(sub_inv == k, row_inv, inverse - below[:, :columns] * row_inv)
    return inverse, lower


def kernel(
    nr, nc, states_ref, jac_hbm, steps_ref, out_ref,
    jac, turned, first, own, gathered, acc, part_send, part_recv, vh, vl, zh, zl, cur, shift, state,
    result, result_recv, sums_send, sums_recv, aug,
    jac_sem, g_send, g_recv, p_send, p_recv, s_send, s_recv, x_send, x_recv, o_send, o_recv,
):
    members, columns, length = states_ref.shape
    cells = nc * length
    chunk = cells // CHUNKS
    share = CHUNKS // nc
    width = vh.shape[0]
    r, c = lax.axis_index("row"), lax.axis_index("col")
    other, beyond = 1 - c, 1 - r
    me = r * nc + c
    count = nr * nc
    home = c == r

    rows = jac.shape[0] // LOADS
    loads = [
        pltpu.make_async_copy(
            jac_hbm.at[i * rows : (i + 1) * rows], jac.at[i * rows : (i + 1) * rows], jac_sem.at[i]
        )
        for i in range(LOADS)
    ]
    for load in loads:
        load.start()
    barrier = pltpu.get_barrier_semaphore()
    for step in range(1, count):
        peer = lax.rem(me + step, count)
        pl.semaphore_signal(
            barrier, inc=1, device_id={"row": peer // nc, "col": lax.rem(peer, nc)},
            device_id_type=MESH,
        )
    for b in range(members):
        rounded = states_ref[b].astype(bf16)
        for k in range(share):
            first[b, k] = rounded[:, k * chunk : (k + 1) * chunk]
    pl.semaphore_wait(barrier, count - 1)

    def remote(src, dst, send, recv, row, col):
        return pltpu.make_async_remote_copy(
            src_ref=src, dst_ref=dst, send_sem=send, recv_sem=recv,
            device_id={"row": row, "col": col}, device_id_type=MESH,
        )

    def opening(row, b, k):
        at = c * share + k
        return remote(
            first.at[b, k], gathered.at[0, b, at, :columns], g_send.at[row, b, at],
            g_recv.at[0, b, at], row, r,
        )

    def opened(b, at):
        return remote(
            first.at[0, 0], gathered.at[0, b, at, :columns], g_send.at[0, b, at],
            g_recv.at[0, b, at], c, other,
        )

    def block(slot, row, k):
        return remote(
            own.at[k], gathered.at[slot, c, k], g_send.at[row, 0, k], g_recv.at[slot, c, k],
            row, r,
        )

    def arrived(slot, b, k):
        return remote(
            own.at[k], gathered.at[slot, b, k], g_send.at[0, 0, k], g_recv.at[slot, b, k], c, other
        )

    def partial(slot):
        return remote(part_send, part_recv.at[slot], p_send, p_recv.at[slot], r, other)

    def sums(slot):
        return remote(sums_send, sums_recv.at[slot], s_send, s_recv.at[slot], beyond, c)

    swap = remote(states_ref.at[other], state.at[c], x_send, x_recv, r, other)

    for b in range(members):
        for k in range(share):
            opening(beyond, b, k).start()
    for b in range(members):
        for k in range(share):
            @pl.when(jnp.logical_not(home))
            def _():
                opening(r, b, k).start()

            @pl.when(home)
            def _():
                gathered[0, b, c * share + k, :columns] = first[b, k]
    swap.start()
    state[c] = states_ref[c]
    for ref in (vh, vl, zh, zl, aug, sums_send):
        ref[...] = jnp.zeros_like(ref)

    def transpose(i, carry):
        at = pl.ds(pl.multiple_of(i * SIDE, SIDE), SIDE)
        for j in range(0, jac.shape[1], SIDE):
            turned[j : j + SIDE, at] = jac[at, j : j + SIDE].T
        return carry

    for i in range(LOADS):
        loads[i].wait()
        lax.fori_loop(i * (rows // SIDE), (i + 1) * (rows // SIDE), transpose, 0)

    def exchange(slot):
        part_send[...] = acc[other, :columns] + acc[other, columns:]
        partial(slot).start()

    def finish(slot):
        return acc[c, :columns] + acc[c, columns:] + part_recv[slot]

    def place(now, slot):
        pair = split(now)
        cur[slot] = now
        vh[:columns], vl[:columns] = pair
        both = jnp.concatenate(pair, axis=0)
        for k in range(CHUNKS):
            own[k] = both[:, k * chunk : (k + 1) * chunk]
        return pair

    def send(slot):
        for k in range(CHUNKS):
            block(slot, beyond, k).start()

        @pl.when(jnp.logical_not(home))
        def _():
            for k in range(CHUNKS):
                block(slot, r, k).start()

        @pl.when(home)
        def _():
            for k in range(CHUNKS):
                gathered[slot, c, k] = own[k]

    def project(i):
        at = slice(i * LANES, (i + 1) * LANES)
        pair = jnp.concatenate([vh[:columns], vl[:columns]], axis=0)
        wide = lax.dot_general(vh[at], pair, NT, preferred_element_type=f32)
        low = lax.dot_general(vl[at], pair[:columns], NT, preferred_element_type=f32)
        sums_send[:, at] = (wide[:, :columns] + (wide[:, columns:] + low)).T

    for k in range(CHUNKS):
        for b in range(members):
            @pl.when(jnp.logical_not(jnp.logical_and(home, k // share == c)))
            def _():
                opened(b, k).wait_recv()

        left = gathered[0, :, k, :columns].reshape(members * columns, chunk)
        for n in range(0, cells, TILE):
            term = lax.dot_general(
                left, turned[k * chunk : (k + 1) * chunk, n : n + TILE], NN,
                preferred_element_type=f32,
            ).reshape(members, columns, TILE)
            if k:
                term = term + acc[:, :columns, n : n + TILE]
            acc[:, :columns, n : n + TILE] = term
    part_send[...] = acc[other, :columns]
    partial(0).start()
    swap.wait()
    for b in range(members):
        for k in range(share):
            opening(beyond, b, k).wait_send()

            @pl.when(jnp.logical_not(home))
            def _():
                opening(r, b, k).wait_send()
    held = jnp.concatenate([state[h] for h in range(nc)], axis=1)
    cube = held * held * held / 3.0
    partial(0).wait()
    place(acc[c, :columns] + part_recv[0] - cube, 0)
    send(1)
    project(0)
    sums(0).start()

    def gather_sums(slot):
        sums(slot).wait()
        total = sums_send[...] + sums_recv[slot]
        lanes = lax.broadcasted_iota(jnp.int32, (columns, width), 1)
        return total, jnp.where(lanes >= columns, total, 0.0)

    def turn(t, carry):
        slot, before = lax.rem(t, 2), lax.rem(t + 1, 2)
        for k in range(CHUNKS):
            for b in range(members):
                @pl.when(jnp.logical_not(jnp.logical_and(home, b == c)))
                def _():
                    arrived(slot, b, k).wait_recv()

            left = gathered[slot, :, k].reshape(members * 2 * columns, chunk)
            for n in range(0, cells, TILE):
                term = lax.dot_general(
                    left, turned[k * chunk : (k + 1) * chunk, n : n + TILE], NN,
                    preferred_element_type=f32,
                ).reshape(members, 2 * columns, TILE)
                if k:
                    term = term + acc[:, :, n : n + TILE]
                acc[:, :, n : n + TILE] = term
        exchange(slot)
        total, projection = gather_sums(before)
        coefficients = split(projection)
        gram = total[:, :columns] - product(coefficients, coefficients, NT)
        inverse, lower = factor(gram, (t * columns, width))
        start = pl.multiple_of((t - 1) * columns, columns)
        aug[pl.ds(start, columns), :] = projection + lower
        inverse = split(inverse)
        shift[...] = product(coefficients, (zh[...], zl[...]), NN)
        for k in range(CHUNKS):
            block(slot, beyond, k).wait_send()

        @pl.when(jnp.logical_not(home))
        def _():
            for k in range(CHUNKS):
                block(slot, r, k).wait_send()

        partial(slot).wait()
        pair = place(product(inverse, split(finish(slot) - shift[...]), NN), slot)
        pl.when(t < BLOCKS)(lambda: send(before))
        here = pl.multiple_of(t * columns, columns)
        zh[pl.ds(here, columns), :], zl[pl.ds(here, columns), :] = pair
        reduced = cur[before] - product(coefficients, (vh[...], vl[...]), NN)
        new = split(product(inverse, split(reduced), NN))
        vh[pl.ds(here, columns), :], vl[pl.ds(here, columns), :] = new
        project(0)
        for i in range(1, width // LANES):
            pl.when((t + 1) * columns > i * LANES)(functools.partial(project, i))
        sums(slot).start()
        return carry

    lax.fori_loop(1, BLOCKS + 1, turn, 0)

    _, projection = gather_sums(BLOCKS % 2)
    aug[BLOCKS * columns : (BLOCKS + 1) * columns] = projection
    x = aug[...] * (steps_ref[c, 0] / 2.0**SQUARINGS)
    xs = split(x)
    x2 = product(xs, xs, NN)
    x2s = split(x2)
    x3 = product(xs, x2s, NN)
    x4 = product(x2s, x2s, NN)
    tail = x / 120.0 + x2 / 720.0 + x3 / 5040.0 + x4 / 40320.0
    aug[...] = x + x2 / 2.0 + x3 / 6.0 + x4 / 24.0 + product(split(x4), split(tail), NN)

    def square(index, carry):
        now = aug[...]
        pair = split(now)
        aug[...] = 2.0 * now + product(pair, pair, NN)
        return carry

    lax.fori_loop(0, SQUARINGS - 1, square, 0)
    now = aug[...]
    top = now[:columns]
    phi = split(2.0 * top + product(split(top), split(now), NN))
    for h in range(nc):
        at = slice(h * length, (h + 1) * length)
        result[h] = product(phi, (vh[:, at], vl[:, at]), NN)
    swap_out = remote(result.at[other], result_recv, o_send, o_recv, r, other)
    swap_out.start()
    out_ref[c] = states_ref[c] + result[c]
    swap_out.wait()
    out_ref[other] = states_ref[other] + result_recv[...]


def local(nr, nc, states, jacobian, step_sizes):
    members, columns, length = states.shape
    assert nr == nc == members == 2
    cells = nc * length
    chunk = cells // CHUNKS
    width = -(-(BLOCKS + 1) * columns // LANES) * LANES
    vmem = pl.BlockSpec(memory_space=pltpu.VMEM)
    dma = pltpu.SemaphoreType.DMA
    return pl.pallas_call(
        functools.partial(kernel, nr, nc),
        out_shape=jax.ShapeDtypeStruct(states.shape, f32),
        in_specs=[vmem, pl.BlockSpec(memory_space=pl.ANY), pl.BlockSpec(memory_space=pltpu.SMEM)],
        out_specs=vmem,
        scratch_shapes=[
            pltpu.VMEM(jacobian.shape, bf16),
            pltpu.VMEM(jacobian.shape[::-1], bf16),
            pltpu.VMEM((members, CHUNKS // nc, columns, chunk), bf16),
            pltpu.VMEM((CHUNKS, 2 * columns, chunk), bf16),
            pltpu.VMEM((2, members, CHUNKS, 2 * columns, chunk), bf16),
            pltpu.VMEM((members, 2 * columns, cells), f32),
            pltpu.VMEM((columns, cells), f32),
            pltpu.VMEM((2, columns, cells), f32),
            pltpu.VMEM((width, cells), bf16),
            pltpu.VMEM((width, cells), bf16),
            pltpu.VMEM((width, cells), bf16),
            pltpu.VMEM((width, cells), bf16),
            pltpu.VMEM((2, columns, cells), f32),
            pltpu.VMEM((columns, cells), f32),
            pltpu.VMEM((nc, columns, length), f32),
            pltpu.VMEM((nc, columns, length), f32),
            pltpu.VMEM((columns, length), f32),
            pltpu.VMEM((columns, width), f32),
            pltpu.VMEM((2, columns, width), f32),
            pltpu.VMEM((width, width), f32),
            dma((LOADS,)), dma((nr, members, CHUNKS)), dma((2, members, CHUNKS)), dma, dma((2,)),
            dma, dma((2,)), dma, dma, dma, dma,
        ],
        compiler_params=pltpu.CompilerParams(
            collective_id=0, has_side_effects=True, vmem_limit_bytes=48 * 2**20
        ),
    )(states, jacobian, step_sizes)


def solution(mesh):
    placed = (P("ens", None, ("row", "col")), P(("ens", "row"), "col"), P("ens", None))
    return jax.shard_map(
        functools.partial(local, mesh.shape["row"], mesh.shape["col"]), mesh=mesh,
        in_specs=placed, out_specs=P("ens", None, ("row", "col")), check_vma=False,
    )
```

```python
import functools

import jax
import jax.numpy as jnp
from jax import lax
from jax.experimental import pallas as pl
from jax.experimental.pallas import tpu as pltpu
from jax.sharding import PartitionSpec as P

BLOCKS = 12
WIDE = 3
SHIFT = -20.5
SQUARINGS = 10
CHUNKS = 8
TILE = 512
SIDE = 256
LOADS = 4
GROUP = 16
LANES = 128
MESH = pl.DeviceIdType.MESH
NN = (((1,), (0,)), ((), ()))
NT = (((1,), (1,)), ((), ()))
f32, bf16 = jnp.float32, jnp.bfloat16


def split(value):
    high = value.astype(bf16)
    return high, (value - high.astype(f32)).astype(bf16)


def product(left, right, dims):
    rows = left[0].shape[0]
    both = jnp.concatenate(left, axis=0)
    wide = lax.dot_general(both, right[0], dims, preferred_element_type=f32)
    low = lax.dot_general(left[0], right[1], dims, preferred_element_type=f32)
    return wide[:rows] + (wide[rows:] + low)


def factor(gram, offset):
    columns = gram.shape[0]
    lanes_inv = lax.broadcasted_iota(jnp.int32, (columns, columns), 1)
    sub_inv = lax.broadcasted_iota(jnp.int32, (columns, columns), 0)
    inverse = jnp.where(lanes_inv == sub_inv, 1.0, 0.0).astype(f32)
    lanes = lax.broadcasted_iota(jnp.int32, (columns, offset[1]), 1)
    lower = jnp.zeros((columns, offset[1]), f32)
    sub = lax.broadcasted_iota(jnp.int32, (columns, LANES), 0)
    for base in range(0, columns, GROUP):
        held = [
            jnp.broadcast_to(gram[:, base + i : base + i + 1], (columns, LANES))
            for i in range(GROUP)
        ]
        for i in range(GROUP):
            k = base + i
            pivot = held[i][k : k + 1, :]
            root = lax.rsqrt(pivot)
            root = root * (1.5 - 0.5 * pivot * root * root)
            column = jnp.where(sub >= k, held[i] * root, 0.0)
            below = jnp.where(sub > k, column, 0.0)
            for later in range(i + 1, GROUP):
                index = base + later
                held[later] = held[later] - below * column[index : index + 1, :]
            wide = jnp.concatenate([column] * (offset[1] // LANES), axis=1)
            lower = jnp.where(lanes == offset[0] + k, wide, lower)
            row = gram[k : k + 1, :] * root[:, :columns]
            row_inv = inverse[k : k + 1, :] * root[:, :columns]
            gram = gram - below[:, :columns] * row
            inverse = jnp.where(sub_inv == k, row_inv, inverse - below[:, :columns] * row_inv)
    return inverse, lower


def kernel(
    nr, nc, states_ref, jac_hbm, steps_ref, out_ref,
    jac, turned, first, own, gathered, acc, part_send, part_recv, vh, vl, zh, zl, cur, shift, state,
    result, result_recv, sums_send, sums_recv, aug,
    jac_sem, g_send, g_recv, p_send, p_recv, s_send, s_recv, x_send, x_recv, o_send, o_recv,
):
    members, columns, length = states_ref.shape
    cells = nc * length
    chunk = cells // CHUNKS
    share = CHUNKS // nc
    width = vh.shape[0]
    r, c = lax.axis_index("row"), lax.axis_index("col")
    other, beyond = 1 - c, 1 - r
    me = r * nc + c
    count = nr * nc
    home = c == r

    rows = jac.shape[0] // LOADS
    loads = [
        pltpu.make_async_copy(
            jac_hbm.at[i * rows : (i + 1) * rows], jac.at[i * rows : (i + 1) * rows], jac_sem.at[i]
        )
        for i in range(LOADS)
    ]
    for load in loads:
        load.start()
    barrier = pltpu.get_barrier_semaphore()
    for step in range(1, count):
        peer = lax.rem(me + step, count)
        pl.semaphore_signal(
            barrier, inc=1, device_id={"row": peer // nc, "col": lax.rem(peer, nc)},
            device_id_type=MESH,
        )
    for b in range(members):
        rounded = states_ref[b].astype(bf16)
        for k in range(share):
            first[b, k] = rounded[:, k * chunk : (k + 1) * chunk]
    pl.semaphore_wait(barrier, count - 1)

    def remote(src, dst, send, recv, row, col):
        return pltpu.make_async_remote_copy(
            src_ref=src, dst_ref=dst, send_sem=send, recv_sem=recv,
            device_id={"row": row, "col": col}, device_id_type=MESH,
        )

    def opening(row, b, k):
        at = c * share + k
        return remote(
            first.at[b, k], gathered.at[0, b, at, :columns], g_send.at[row, b, at],
            g_recv.at[0, b, at], row, r,
        )

    def opened(b, at):
        return remote(
            first.at[0, 0], gathered.at[0, b, at, :columns], g_send.at[0, b, at],
            g_recv.at[0, b, at], c, other,
        )

    def block(slot, row, k, parts):
        return remote(
            own.at[k, : parts * columns], gathered.at[slot, c, k, : parts * columns],
            g_send.at[row, 0, k], g_recv.at[slot, c, k], row, r,
        )

    def arrived(slot, b, k, parts):
        return remote(
            own.at[k, : parts * columns], gathered.at[slot, b, k, : parts * columns],
            g_send.at[0, 0, k], g_recv.at[slot, b, k], c, other,
        )

    def partial(slot):
        return remote(part_send, part_recv.at[slot], p_send, p_recv.at[slot], r, other)

    def sums(slot):
        return remote(sums_send, sums_recv.at[slot], s_send, s_recv.at[slot], beyond, c)

    swap = remote(states_ref.at[other], state.at[c], x_send, x_recv, r, other)

    for b in range(members):
        for k in range(share):
            opening(beyond, b, k).start()
    for b in range(members):
        for k in range(share):
            @pl.when(jnp.logical_not(home))
            def _():
                opening(r, b, k).start()

            @pl.when(home)
            def _():
                gathered[0, b, c * share + k, :columns] = first[b, k]
    swap.start()
    state[c] = states_ref[c]
    for ref in (vh, vl, zh, zl, aug, sums_send):
        ref[...] = jnp.zeros_like(ref)

    def transpose(i, carry):
        at = pl.ds(pl.multiple_of(i * SIDE, SIDE), SIDE)
        for j in range(0, jac.shape[1], SIDE):
            turned[j : j + SIDE, at] = jac[at, j : j + SIDE].T
        return carry

    for i in range(LOADS):
        loads[i].wait()
        lax.fori_loop(i * (rows // SIDE), (i + 1) * (rows // SIDE), transpose, 0)

    def weigh(parts):
        if parts == 2:
            return lambda b: acc[b, :columns] + acc[b, columns:]
        return lambda b: acc[b, :columns]

    def place(now, slot):
        pair = split(now)
        cur[slot] = now
        vh[:columns], vl[:columns] = pair
        both = jnp.concatenate(pair, axis=0)
        for k in range(CHUNKS):
            own[k] = both[:, k * chunk : (k + 1) * chunk]
        return pair

    def send(slot, parts):
        for k in range(CHUNKS):
            block(slot, beyond, k, parts).start()

        @pl.when(jnp.logical_not(home))
        def _():
            for k in range(CHUNKS):
                block(slot, r, k, parts).start()

        @pl.when(home)
        def _():
            for k in range(CHUNKS):
                gathered[slot, c, k, : parts * columns] = own[k, : parts * columns]

    def project(i):
        at = slice(i * LANES, (i + 1) * LANES)
        pair = jnp.concatenate([vh[:columns], vl[:columns]], axis=0)
        wide = lax.dot_general(vh[at], pair, NT, preferred_element_type=f32)
        low = lax.dot_general(vl[at], pair[:columns], NT, preferred_element_type=f32)
        sums_send[:, at] = (wide[:, :columns] + (wide[:, columns:] + low)).T

    for k in range(CHUNKS):
        for b in range(members):
            @pl.when(jnp.logical_not(jnp.logical_and(home, k // share == c)))
            def _():
                opened(b, k).wait_recv()

        left = gathered[0, :, k, :columns].reshape(members * columns, chunk)
        for n in range(0, cells, TILE):
            term = lax.dot_general(
                left, turned[k * chunk : (k + 1) * chunk, n : n + TILE], NN,
                preferred_element_type=f32,
            ).reshape(members, columns, TILE)
            if k:
                term = term + acc[:, :columns, n : n + TILE]
            acc[:, :columns, n : n + TILE] = term
    part_send[...] = acc[other, :columns]
    partial(0).start()
    swap.wait()
    for b in range(members):
        for k in range(share):
            opening(beyond, b, k).wait_send()

            @pl.when(jnp.logical_not(home))
            def _():
                opening(r, b, k).wait_send()
    held = jnp.concatenate([state[h] for h in range(nc)], axis=1)
    cube = held * held * held / 3.0
    partial(0).wait()
    place(acc[c, :columns] + part_recv[0] - cube, 0)
    send(1, 2)
    project(0)
    sums(0).start()

    def keep(t, rows):
        at = pl.multiple_of(t * columns, columns)
        lanes = lax.broadcasted_iota(jnp.int32, (columns, width), 1)
        sub = lax.broadcasted_iota(jnp.int32, (columns, width), 0) + at
        on = jnp.logical_and(lanes == sub, lanes >= columns)
        aug[pl.ds(at, columns), :] = rows + jnp.where(on, SHIFT, 0.0)

    def gather_sums(slot):
        sums(slot).wait()
        total = sums_send[...] + sums_recv[slot]
        lanes = lax.broadcasted_iota(jnp.int32, (columns, width), 1)
        return total, jnp.where(lanes >= columns, total, 0.0)

    def turn(parts, after, t, carry):
        slot, before = lax.rem(t, 2), lax.rem(t + 1, 2)
        for k in range(CHUNKS):
            for b in range(members):
                @pl.when(jnp.logical_not(jnp.logical_and(home, b == c)))
                def _():
                    arrived(slot, b, k, parts).wait_recv()

            left = gathered[slot, :, k, : parts * columns].reshape(members * parts * columns, chunk)
            for n in range(0, cells, TILE):
                term = lax.dot_general(
                    left, turned[k * chunk : (k + 1) * chunk, n : n + TILE], NN,
                    preferred_element_type=f32,
                ).reshape(members, parts * columns, TILE)
                if k:
                    term = term + acc[:, : parts * columns, n : n + TILE]
                acc[:, : parts * columns, n : n + TILE] = term
        weighed = weigh(parts)
        part_send[...] = weighed(other)
        partial(slot).start()
        total, projection = gather_sums(before)
        coefficients = split(projection)
        gram = total[:, :columns] - product(coefficients, coefficients, NT)
        inverse, lower = factor(gram, (t * columns, width))
        keep(t - 1, projection + lower)
        inverse = split(inverse)
        shift[...] = product(coefficients, (zh[...], zl[...]), NN) + SHIFT * cur[before]
        for k in range(CHUNKS):
            block(slot, beyond, k, parts).wait_send()

        @pl.when(jnp.logical_not(home))
        def _():
            for k in range(CHUNKS):
                block(slot, r, k, parts).wait_send()

        partial(slot).wait()
        image = weighed(c) + part_recv[slot] - shift[...]
        pair = place(product(inverse, split(image), NN), slot)
        if after:
            send(before, after)
        here = pl.multiple_of(t * columns, columns)
        zh[pl.ds(here, columns), :], zl[pl.ds(here, columns), :] = pair
        reduced = cur[before] - product(coefficients, (vh[...], vl[...]), NN)
        new = split(product(inverse, split(reduced), NN))
        vh[pl.ds(here, columns), :], vl[pl.ds(here, columns), :] = new
        project(0)
        for i in range(1, width // LANES):
            pl.when((t + 1) * columns > i * LANES)(functools.partial(project, i))
        sums(slot).start()
        return carry

    lax.fori_loop(1, WIDE, functools.partial(turn, 2, 2), 0)
    turn(2, 1, WIDE, 0)
    lax.fori_loop(WIDE + 1, BLOCKS, functools.partial(turn, 1, 1), 0)
    turn(1, 0, BLOCKS, 0)

    _, projection = gather_sums(BLOCKS % 2)
    keep(BLOCKS, projection)
    x = aug[...] * (steps_ref[c, 0] / 2.0**SQUARINGS)
    xs = split(x)
    x2 = product(xs, xs, NN)
    x2s = split(x2)
    x3 = product(xs, x2s, NN)
    x4 = product(x2s, x2s, NN)
    tail = x / 120.0 + x2 / 720.0 + x3 / 5040.0 + x4 / 40320.0
    aug[...] = x + x2 / 2.0 + x3 / 6.0 + x4 / 24.0 + product(split(x4), split(tail), NN)

    def square(index, carry):
        now = aug[...]
        pair = split(now)
        aug[...] = 2.0 * now + product(pair, pair, NN)
        return carry

    lax.fori_loop(0, SQUARINGS - 1, square, 0)
    now = aug[...]
    top = now[:columns]
    phi = split(2.0 * top + product(split(top), split(now), NN))
    for h in range(nc):
        at = slice(h * length, (h + 1) * length)
        result[h] = product(phi, (vh[:, at], vl[:, at]), NN)
    swap_out = remote(result.at[other], result_recv, o_send, o_recv, r, other)
    swap_out.start()
    out_ref[c] = states_ref[c] + result[c]
    swap_out.wait()
    out_ref[other] = states_ref[other] + result_recv[...]


def local(nr, nc, states, jacobian, step_sizes):
    members, columns, length = states.shape
    assert nr == nc == members == 2
    cells = nc * length
    chunk = cells // CHUNKS
    width = -(-(BLOCKS + 1) * columns // LANES) * LANES
    vmem = pl.BlockSpec(memory_space=pltpu.VMEM)
    dma = pltpu.SemaphoreType.DMA
    return pl.pallas_call(
        functools.partial(kernel, nr, nc),
        out_shape=jax.ShapeDtypeStruct(states.shape, f32),
        in_specs=[vmem, pl.BlockSpec(memory_space=pl.ANY), pl.BlockSpec(memory_space=pltpu.SMEM)],
        out_specs=vmem,
        scratch_shapes=[
            pltpu.VMEM(jacobian.shape, bf16),
            pltpu.VMEM(jacobian.shape[::-1], bf16),
            pltpu.VMEM((members, CHUNKS // nc, columns, chunk), bf16),
            pltpu.VMEM((CHUNKS, 2 * columns, chunk), bf16),
            pltpu.VMEM((2, members, CHUNKS, 2 * columns, chunk), bf16),
            pltpu.VMEM((members, 2 * columns, cells), f32),
            pltpu.VMEM((columns, cells), f32),
            pltpu.VMEM((2, columns, cells), f32),
            pltpu.VMEM((width, cells), bf16),
            pltpu.VMEM((width, cells), bf16),
            pltpu.VMEM((width, cells), bf16),
            pltpu.VMEM((width, cells), bf16),
            pltpu.VMEM((2, columns, cells), f32),
            pltpu.VMEM((columns, cells), f32),
            pltpu.VMEM((nc, columns, length), f32),
            pltpu.VMEM((nc, columns, length), f32),
            pltpu.VMEM((columns, length), f32),
            pltpu.VMEM((columns, width), f32),
            pltpu.VMEM((2, columns, width), f32),
            pltpu.VMEM((width, width), f32),
            dma((LOADS,)), dma((nr, members, CHUNKS)), dma((2, members, CHUNKS)), dma, dma((2,)),
            dma, dma((2,)), dma, dma, dma, dma,
        ],
        compiler_params=pltpu.CompilerParams(
            collective_id=0, has_side_effects=True, vmem_limit_bytes=48 * 2**20
        ),
    )(states, jacobian, step_sizes)


def solution(mesh):
    placed = (P("ens", None, ("row", "col")), P(("ens", "row"), "col"), P("ens", None))
    return jax.shard_map(
        functools.partial(local, mesh.shape["row"], mesh.shape["col"]), mesh=mesh,
        in_specs=placed, out_specs=P("ens", None, ("row", "col")), check_vma=False,
    )
```

```python
import functools

import jax
import jax.numpy as jnp
from jax import lax
from jax.experimental import pallas as pl
from jax.experimental.pallas import tpu as pltpu
from jax.sharding import PartitionSpec as P

BLOCKS = 12
WIDE = 1
SHIFT = -20.5
STEP = 128
SQUARINGS = 10
CHUNKS = 8
TILE = 512
SIDE = 256
LOADS = 4
GROUP = 16
LANES = 128
MESH = pl.DeviceIdType.MESH
NN = (((1,), (0,)), ((), ()))
NT = (((1,), (1,)), ((), ()))
f32, bf16 = jnp.float32, jnp.bfloat16


def split(value):
    high = value.astype(bf16)
    return high, (value - high.astype(f32)).astype(bf16)


def product(left, right, dims):
    rows = left[0].shape[0]
    both = jnp.concatenate(left, axis=0)
    wide = lax.dot_general(both, right[0], dims, preferred_element_type=f32)
    low = lax.dot_general(left[0], right[1], dims, preferred_element_type=f32)
    return wide[:rows] + (wide[rows:] + low)


def factor(gram, offset):
    columns = gram.shape[0]
    lanes_inv = lax.broadcasted_iota(jnp.int32, (columns, columns), 1)
    sub_inv = lax.broadcasted_iota(jnp.int32, (columns, columns), 0)
    inverse = jnp.where(lanes_inv == sub_inv, 1.0, 0.0).astype(f32)
    lanes = lax.broadcasted_iota(jnp.int32, (columns, offset[1]), 1)
    lower = jnp.zeros((columns, offset[1]), f32)
    sub = lax.broadcasted_iota(jnp.int32, (columns, LANES), 0)
    for base in range(0, columns, GROUP):
        held = [
            jnp.broadcast_to(gram[:, base + i : base + i + 1], (columns, LANES))
            for i in range(GROUP)
        ]
        for i in range(GROUP):
            k = base + i
            pivot = held[i][k : k + 1, :]
            root = lax.rsqrt(pivot)
            root = root * (1.5 - 0.5 * pivot * root * root)
            column = jnp.where(sub >= k, held[i] * root, 0.0)
            below = jnp.where(sub > k, column, 0.0)
            for later in range(i + 1, GROUP):
                index = base + later
                held[later] = held[later] - below * column[index : index + 1, :]
            wide = jnp.concatenate([column] * (offset[1] // LANES), axis=1)
            lower = jnp.where(lanes == offset[0] + k, wide, lower)
            row = gram[k : k + 1, :] * root[:, :columns]
            row_inv = inverse[k : k + 1, :] * root[:, :columns]
            gram = gram - below[:, :columns] * row
            inverse = jnp.where(sub_inv == k, row_inv, inverse - below[:, :columns] * row_inv)
    return inverse, lower


def kernel(
    nr, nc, states_hbm, jac_hbm, steps_hbm, out_ref, states_ref, steps_ref,
    jac, turned, first, own, gathered, acc, part_send, part_recv, vh, vl, zh, zl, cur, shift, state,
    result, result_recv, sums_send, sums_recv, aug,
    in_sem, jac_sem, g_send, g_recv, p_send, p_recv, s_send, s_recv, x_send, x_recv, o_send, o_recv,
):
    members, columns, length = states_hbm.shape
    cells = nc * length
    chunk = cells // CHUNKS
    share = CHUNKS // nc
    width = vh.shape[0]
    r, c = lax.axis_index("row"), lax.axis_index("col")
    other, beyond = 1 - c, 1 - r
    me = r * nc + c
    count = nr * nc
    home = c == r

    rows = jac.shape[0] // LOADS
    loads = [
        pltpu.make_async_copy(
            jac_hbm.at[i * rows : (i + 1) * rows], jac.at[i * rows : (i + 1) * rows], jac_sem.at[i]
        )
        for i in range(LOADS)
    ]
    load_states = pltpu.make_async_copy(states_hbm, states_ref, in_sem.at[0])
    load_steps = pltpu.make_async_copy(steps_hbm, steps_ref, in_sem.at[1])
    load_states.start()
    load_steps.start()
    for load in loads:
        load.start()
    barrier = pltpu.get_barrier_semaphore()
    for step in range(1, count):
        peer = lax.rem(me + step, count)
        pl.semaphore_signal(
            barrier, inc=1, device_id={"row": peer // nc, "col": lax.rem(peer, nc)},
            device_id_type=MESH,
        )
    load_states.wait()
    for b in range(members):
        rounded = states_ref[b].astype(bf16)
        for k in range(share):
            first[b, k] = rounded[:, k * chunk : (k + 1) * chunk]
    pl.semaphore_wait(barrier, count - 1)

    def remote(src, dst, send, recv, row, col):
        return pltpu.make_async_remote_copy(
            src_ref=src, dst_ref=dst, send_sem=send, recv_sem=recv,
            device_id={"row": row, "col": col}, device_id_type=MESH,
        )

    def opening(row, b, k):
        at = c * share + k
        return remote(
            first.at[b, k], gathered.at[0, b, at, :columns], g_send.at[row, b, at],
            g_recv.at[0, b, at], row, r,
        )

    def opened(b, at):
        return remote(
            first.at[0, 0], gathered.at[0, b, at, :columns], g_send.at[0, b, at],
            g_recv.at[0, b, at], c, other,
        )

    def block(slot, row, k, parts):
        return remote(
            own.at[k, : parts * columns], gathered.at[slot, c, k, : parts * columns],
            g_send.at[row, 0, k], g_recv.at[slot, c, k], row, r,
        )

    def arrived(slot, b, k, parts):
        return remote(
            own.at[k, : parts * columns], gathered.at[slot, b, k, : parts * columns],
            g_send.at[0, 0, k], g_recv.at[slot, b, k], c, other,
        )

    def partial(slot):
        return remote(part_send, part_recv.at[slot], p_send, p_recv.at[slot], r, other)

    def sums(slot):
        return remote(sums_send, sums_recv.at[slot], s_send, s_recv.at[slot], beyond, c)

    swap = remote(states_ref.at[other], state.at[c], x_send, x_recv, r, other)

    for b in range(members):
        for k in range(share):
            opening(beyond, b, k).start()
    for b in range(members):
        for k in range(share):
            @pl.when(jnp.logical_not(home))
            def _():
                opening(r, b, k).start()

            @pl.when(home)
            def _():
                gathered[0, b, c * share + k, :columns] = first[b, k]
    swap.start()
    state[c] = states_ref[c]
    for ref in (vh, vl, zh, zl, aug, sums_send):
        ref[...] = jnp.zeros_like(ref)

    def transpose(i, carry):
        at = pl.ds(pl.multiple_of(i * SIDE, SIDE), SIDE)
        for j in range(0, jac.shape[1], SIDE):
            turned[j : j + SIDE, at] = jac[at, j : j + SIDE].T
        return carry

    for i in range(LOADS):
        loads[i].wait()
        lax.fori_loop(i * (rows // SIDE), (i + 1) * (rows // SIDE), transpose, 0)

    def weigh(parts):
        if parts == 2:
            return lambda b: acc[b, :columns] + acc[b, columns:]
        return lambda b: acc[b, :columns]

    def place(now, slot):
        pair = split(now)
        cur[slot] = now
        vh[:columns], vl[:columns] = pair
        both = jnp.concatenate(pair, axis=0)
        for k in range(CHUNKS):
            own[k] = both[:, k * chunk : (k + 1) * chunk]
        return pair

    def send(slot, parts):
        for k in range(CHUNKS):
            block(slot, beyond, k, parts).start()

        @pl.when(jnp.logical_not(home))
        def _():
            for k in range(CHUNKS):
                block(slot, r, k, parts).start()

        @pl.when(home)
        def _():
            for k in range(CHUNKS):
                gathered[slot, c, k, : parts * columns] = own[k, : parts * columns]

    def project(height):
        at = slice(0, height)
        pair = jnp.concatenate([vh[:columns], vl[:columns]], axis=0)
        wide = lax.dot_general(vh[at], pair, NT, preferred_element_type=f32)
        low = lax.dot_general(vl[at], pair[:columns], NT, preferred_element_type=f32)
        sums_send[:, at] = (wide[:, :columns] + (wide[:, columns:] + low)).T

    for k in range(CHUNKS):
        for b in range(members):
            @pl.when(jnp.logical_not(jnp.logical_and(home, k // share == c)))
            def _():
                opened(b, k).wait_recv()

        left = gathered[0, :, k, :columns].reshape(members * columns, chunk)
        for n in range(0, cells, TILE):
            term = lax.dot_general(
                left, turned[k * chunk : (k + 1) * chunk, n : n + TILE], NN,
                preferred_element_type=f32,
            ).reshape(members, columns, TILE)
            if k:
                term = term + acc[:, :columns, n : n + TILE]
            acc[:, :columns, n : n + TILE] = term
    part_send[...] = acc[other, :columns]
    partial(0).start()
    swap.wait()
    for b in range(members):
        for k in range(share):
            opening(beyond, b, k).wait_send()

            @pl.when(jnp.logical_not(home))
            def _():
                opening(r, b, k).wait_send()
    held = jnp.concatenate([state[h] for h in range(nc)], axis=1)
    cube = held * held * held / 3.0
    partial(0).wait()
    place(acc[c, :columns] + part_recv[0] - cube, 0)
    send(1, 2)
    project(LANES)
    sums(0).start()

    def keep(t, rows):
        at = pl.multiple_of(t * columns, columns)
        lanes = lax.broadcasted_iota(jnp.int32, (columns, width), 1)
        sub = lax.broadcasted_iota(jnp.int32, (columns, width), 0) + at
        on = jnp.logical_and(lanes == sub, lanes >= columns)
        aug[pl.ds(at, columns), :] = rows + jnp.where(on, SHIFT, 0.0)

    def gather_sums(slot):
        sums(slot).wait()
        total = sums_send[...] + sums_recv[slot]
        lanes = lax.broadcasted_iota(jnp.int32, (columns, width), 1)
        return total, jnp.where(lanes >= columns, total, 0.0)

    def turn(parts, after, height, t, carry):
        slot, before = lax.rem(t, 2), lax.rem(t + 1, 2)
        for k in range(CHUNKS):
            for b in range(members):
                @pl.when(jnp.logical_not(jnp.logical_and(home, b == c)))
                def _():
                    arrived(slot, b, k, parts).wait_recv()

            left = gathered[slot, :, k, : parts * columns].reshape(members * parts * columns, chunk)
            for n in range(0, cells, TILE):
                term = lax.dot_general(
                    left, turned[k * chunk : (k + 1) * chunk, n : n + TILE], NN,
                    preferred_element_type=f32,
                ).reshape(members, parts * columns, TILE)
                if k:
                    term = term + acc[:, : parts * columns, n : n + TILE]
                acc[:, : parts * columns, n : n + TILE] = term
        weighed = weigh(parts)
        part_send[...] = weighed(other)
        partial(slot).start()
        total, projection = gather_sums(before)
        coefficients = split(projection[:, :height])
        gram = total[:, :columns] - product(coefficients, coefficients, NT)
        inverse, lower = factor(gram, (t * columns, width))
        keep(t - 1, projection + lower)
        inverse = split(inverse)
        shift[...] = product(coefficients, (zh[:height], zl[:height]), NN) + SHIFT * cur[before]
        for k in range(CHUNKS):
            block(slot, beyond, k, parts).wait_send()

        @pl.when(jnp.logical_not(home))
        def _():
            for k in range(CHUNKS):
                block(slot, r, k, parts).wait_send()

        partial(slot).wait()
        image = weighed(c) + part_recv[slot] - shift[...]
        pair = place(product(inverse, split(image), NN), slot)
        if after:
            send(before, after)
        here = pl.multiple_of(t * columns, columns)
        zh[pl.ds(here, columns), :], zl[pl.ds(here, columns), :] = pair
        reduced = cur[before] - product(coefficients, (vh[:height], vl[:height]), NN)
        new = split(product(inverse, split(reduced), NN))
        vh[pl.ds(here, columns), :], vl[pl.ds(here, columns), :] = new
        project(height)
        sums(slot).start()
        return carry

    first_turn = 1
    while first_turn <= BLOCKS:
        height = -(-(first_turn + 1) * columns // STEP) * STEP
        parts = 2 if first_turn <= WIDE else 1
        after = 0 if first_turn == BLOCKS else 2 if first_turn < WIDE else 1
        last_turn = first_turn
        if first_turn not in (WIDE, BLOCKS):
            last_turn = min(height // columns - 1, BLOCKS - 1)
            if first_turn < WIDE:
                last_turn = min(last_turn, WIDE - 1)
        body = functools.partial(turn, parts, after, height)
        if first_turn == last_turn:
            body(first_turn, 0)
        else:
            lax.fori_loop(first_turn, last_turn + 1, body, 0)
        first_turn = last_turn + 1

    _, projection = gather_sums(BLOCKS % 2)
    keep(BLOCKS, projection)
    load_steps.wait()
    x = aug[...] * (steps_ref[c, 0] / 2.0**SQUARINGS)
    xs = split(x)
    x2 = product(xs, xs, NN)
    x2s = split(x2)
    x3 = product(xs, x2s, NN)
    x4 = product(x2s, x2s, NN)
    tail = x / 120.0 + x2 / 720.0 + x3 / 5040.0 + x4 / 40320.0
    aug[...] = x + x2 / 2.0 + x3 / 6.0 + x4 / 24.0 + product(split(x4), split(tail), NN)

    def square(index, carry):
        now = aug[...]
        pair = split(now)
        aug[...] = 2.0 * now + product(pair, pair, NN)
        return carry

    lax.fori_loop(0, SQUARINGS - 1, square, 0)
    now = aug[...]
    top = now[:columns]
    phi = split(2.0 * top + product(split(top), split(now), NN))
    swap_out = remote(result.at[other], result_recv, o_send, o_recv, r, other)

    def advance(h):
        at = pl.ds(pl.multiple_of(h * length, length), length)
        result[h] = product(phi, (vh[:, at], vl[:, at]), NN)

    advance(other)
    swap_out.start()
    advance(c)
    out_ref[c] = states_ref[c] + result[c]
    swap_out.wait()
    out_ref[other] = states_ref[other] + result_recv[...]


def local(nr, nc, states, jacobian, step_sizes):
    members, columns, length = states.shape
    assert nr == nc == members == 2
    cells = nc * length
    chunk = cells // CHUNKS
    width = -(-(BLOCKS + 1) * columns // LANES) * LANES
    vmem = pl.BlockSpec(memory_space=pltpu.VMEM)
    dma = pltpu.SemaphoreType.DMA
    return pl.pallas_call(
        functools.partial(kernel, nr, nc),
        out_shape=jax.ShapeDtypeStruct(states.shape, f32),
        in_specs=[pl.BlockSpec(memory_space=pl.ANY)] * 3,
        out_specs=vmem,
        scratch_shapes=[
            pltpu.VMEM(states.shape, f32),
            pltpu.SMEM(step_sizes.shape, f32),
            pltpu.VMEM(jacobian.shape, bf16),
            pltpu.VMEM(jacobian.shape[::-1], bf16),
            pltpu.VMEM((members, CHUNKS // nc, columns, chunk), bf16),
            pltpu.VMEM((CHUNKS, 2 * columns, chunk), bf16),
            pltpu.VMEM((2, members, CHUNKS, 2 * columns, chunk), bf16),
            pltpu.VMEM((members, 2 * columns, cells), f32),
            pltpu.VMEM((columns, cells), f32),
            pltpu.VMEM((2, columns, cells), f32),
            pltpu.VMEM((width, cells), bf16),
            pltpu.VMEM((width, cells), bf16),
            pltpu.VMEM((width, cells), bf16),
            pltpu.VMEM((width, cells), bf16),
            pltpu.VMEM((2, columns, cells), f32),
            pltpu.VMEM((columns, cells), f32),
            pltpu.VMEM((nc, columns, length), f32),
            pltpu.VMEM((nc, columns, length), f32),
            pltpu.VMEM((columns, length), f32),
            pltpu.VMEM((columns, width), f32),
            pltpu.VMEM((2, columns, width), f32),
            pltpu.VMEM((width, width), f32),
            dma((2,)), dma((LOADS,)), dma((nr, members, CHUNKS)), dma((2, members, CHUNKS)), dma, dma((2,)),
            dma, dma((2,)), dma, dma, dma, dma,
        ],
        compiler_params=pltpu.CompilerParams(
            collective_id=0, has_side_effects=True, vmem_limit_bytes=48 * 2**20
        ),
    )(states, jacobian, step_sizes)


def solution(mesh):
    placed = (P("ens", None, ("row", "col")), P(("ens", "row"), "col"), P("ens", None))
    return jax.shard_map(
        functools.partial(local, mesh.shape["row"], mesh.shape["col"]), mesh=mesh,
        in_specs=placed, out_specs=P("ens", None, ("row", "col")), check_vma=False,
    )
```

```python
import functools

import jax
import jax.numpy as jnp
from jax import lax
from jax.experimental import pallas as pl
from jax.experimental.pallas import tpu as pltpu
from jax.sharding import PartitionSpec as P

BLOCKS = 12
WIDE = 1
SHIFT = -20.5
STEP = 128
SQUARINGS = 10
CHUNKS = 16
TILE = 512
SIDE = 256
LOADS = 4
GROUP = 16
LANES = 128
MESH = pl.DeviceIdType.MESH
NN = (((1,), (0,)), ((), ()))
NT = (((1,), (1,)), ((), ()))
f32, bf16 = jnp.float32, jnp.bfloat16


def split(value):
    high = value.astype(bf16)
    return high, (value - high.astype(f32)).astype(bf16)


def product(left, right, dims):
    rows = left[0].shape[0]
    both = jnp.concatenate(left, axis=0)
    wide = lax.dot_general(both, right[0], dims, preferred_element_type=f32)
    low = lax.dot_general(left[0], right[1], dims, preferred_element_type=f32)
    return wide[:rows] + (wide[rows:] + low)


def factor(gram, offset):
    columns = gram.shape[0]
    lanes_inv = lax.broadcasted_iota(jnp.int32, (columns, columns), 1)
    sub_inv = lax.broadcasted_iota(jnp.int32, (columns, columns), 0)
    inverse = jnp.where(lanes_inv == sub_inv, 1.0, 0.0).astype(f32)
    lanes = lax.broadcasted_iota(jnp.int32, (columns, offset[1]), 1)
    lower = jnp.zeros((columns, offset[1]), f32)
    sub = lax.broadcasted_iota(jnp.int32, (columns, LANES), 0)
    for base in range(0, columns, GROUP):
        held = [
            jnp.broadcast_to(gram[:, base + i : base + i + 1], (columns, LANES))
            for i in range(GROUP)
        ]
        for i in range(GROUP):
            k = base + i
            pivot = held[i][k : k + 1, :]
            root = lax.rsqrt(pivot)
            root = root * (1.5 - 0.5 * pivot * root * root)
            column = jnp.where(sub >= k, held[i] * root, 0.0)
            below = jnp.where(sub > k, column, 0.0)
            for later in range(i + 1, GROUP):
                index = base + later
                held[later] = held[later] - below * column[index : index + 1, :]
            wide = jnp.concatenate([column] * (offset[1] // LANES), axis=1)
            lower = jnp.where(lanes == offset[0] + k, wide, lower)
            row = gram[k : k + 1, :] * root[:, :columns]
            row_inv = inverse[k : k + 1, :] * root[:, :columns]
            gram = gram - below[:, :columns] * row
            inverse = jnp.where(sub_inv == k, row_inv, inverse - below[:, :columns] * row_inv)
    return inverse, lower


def kernel(
    nr, nc, states_hbm, jac_hbm, steps_hbm, out_ref, states_ref, steps_ref,
    jac, turned, first, own, gathered, acc, part_send, part_recv, vh, vl, zh, zl, cur, shift, state,
    result, result_recv, sums_send, sums_recv, aug,
    in_sem, jac_sem, g_send, g_recv, b_send, d_send, d_recv, p_send, p_recv, s_send, s_recv, x_send, x_recv, o_send, o_recv,
):
    members, columns, length = states_hbm.shape
    cells = nc * length
    chunk = cells // CHUNKS
    share = CHUNKS // nc
    width = vh.shape[0]
    r, c = lax.axis_index("row"), lax.axis_index("col")
    other, beyond = 1 - c, 1 - r
    me = r * nc + c
    count = nr * nc
    home = c == r

    rows = jac.shape[0] // LOADS
    loads = [
        pltpu.make_async_copy(
            jac_hbm.at[i * rows : (i + 1) * rows], jac.at[i * rows : (i + 1) * rows], jac_sem.at[i]
        )
        for i in range(LOADS)
    ]
    load_states = pltpu.make_async_copy(states_hbm, states_ref, in_sem.at[0])
    load_steps = pltpu.make_async_copy(steps_hbm, steps_ref, in_sem.at[1])
    load_states.start()
    load_steps.start()
    for load in loads:
        load.start()
    barrier = pltpu.get_barrier_semaphore()
    for step in range(1, count):
        peer = lax.rem(me + step, count)
        pl.semaphore_signal(
            barrier, inc=1, device_id={"row": peer // nc, "col": lax.rem(peer, nc)},
            device_id_type=MESH,
        )
    load_states.wait()
    for b in range(members):
        rounded = states_ref[b].astype(bf16)
        for k in range(share):
            first[b, k] = rounded[:, k * chunk : (k + 1) * chunk]
    pl.semaphore_wait(barrier, count - 1)

    def remote(src, dst, send, recv, row, col):
        return pltpu.make_async_remote_copy(
            src_ref=src, dst_ref=dst, send_sem=send, recv_sem=recv,
            device_id={"row": row, "col": col}, device_id_type=MESH,
        )

    def opening(row, b, k):
        at = c * share + k
        return remote(
            first.at[b, k], gathered.at[0, b, at, :columns], g_send.at[row, b, at],
            g_recv.at[0, b, at], row, r,
        )

    def opened(b, at):
        return remote(
            first.at[0, 0], gathered.at[0, b, at, :columns], g_send.at[0, b, at],
            g_recv.at[0, b, at], c, other,
        )

    def block(slot, k, parts):
        at = slice(0, parts * columns)
        return remote(
            own.at[slot, k, at], gathered.at[slot, c, k, at], b_send.at[slot, k],
            g_recv.at[slot, c, k], beyond, r,
        )

    def arrived(slot, b, k, parts):
        at = slice(0, parts * columns)
        return remote(
            own.at[slot, k, at], gathered.at[slot, b, k, at], b_send.at[slot, k],
            g_recv.at[slot, b, k], beyond, r,
        )

    def whole(slot, owner, parts):
        at = slice(0, parts * columns)
        return remote(
            own.at[slot, :, at], gathered.at[slot, owner, :, at], d_send.at[slot],
            d_recv.at[slot], r, other,
        )

    def partial(slot, parts):
        source = part_send if parts == 2 else acc.at[other, :columns]
        return remote(source, part_recv.at[slot], p_send, p_recv.at[slot], r, other)

    def sums(slot):
        return remote(sums_send, sums_recv.at[slot], s_send, s_recv.at[slot], beyond, c)

    swap = remote(states_ref.at[other], state.at[c], x_send, x_recv, r, other)

    for b in range(members):
        for k in range(share):
            opening(beyond, b, k).start()
    for b in range(members):
        for k in range(share):
            @pl.when(jnp.logical_not(home))
            def _():
                opening(r, b, k).start()

            @pl.when(home)
            def _():
                gathered[0, b, c * share + k, :columns] = first[b, k]
    swap.start()
    state[c] = states_ref[c]
    for ref in (vh, vl, zh, zl, aug, sums_send):
        ref[...] = jnp.zeros_like(ref)

    def transpose(i, carry):
        at = pl.ds(pl.multiple_of(i * SIDE, SIDE), SIDE)
        for j in range(0, jac.shape[1], SIDE):
            turned[j : j + SIDE, at] = jac[at, j : j + SIDE].T
        return carry

    for i in range(LOADS):
        loads[i].wait()
        lax.fori_loop(i * (rows // SIDE), (i + 1) * (rows // SIDE), transpose, 0)

    def weigh(parts):
        if parts == 2:
            return lambda b: acc[b, :columns] + acc[b, columns:]
        return lambda b: acc[b, :columns]

    def place(now, slot, out):
        pair = split(now)
        cur[slot] = now
        vh[:columns], vl[:columns] = pair
        both = jnp.concatenate(pair, axis=0)
        for k in range(CHUNKS):
            own[out, k] = both[:, k * chunk : (k + 1) * chunk]
        return pair

    def send(slot, parts):
        for k in range(CHUNKS):
            block(slot, k, parts).start()

        @pl.when(jnp.logical_not(home))
        def _():
            whole(slot, c, parts).start()

        @pl.when(home)
        def _():
            at = slice(0, parts * columns)
            gathered[slot, c, :, at] = own[slot, :, at]

    def project(height):
        at = slice(0, height)
        pair = jnp.concatenate([vh[:columns], vl[:columns]], axis=0)
        wide = lax.dot_general(vh[at], pair, NT, preferred_element_type=f32)
        low = lax.dot_general(vl[at], pair[:columns], NT, preferred_element_type=f32)
        sums_send[:, at] = (wide[:, :columns] + (wide[:, columns:] + low)).T

    for k in range(CHUNKS):
        for b in range(members):
            @pl.when(jnp.logical_not(jnp.logical_and(home, k // share == c)))
            def _():
                opened(b, k).wait_recv()

        left = gathered[0, :, k, :columns].reshape(members * columns, chunk)
        for n in range(0, cells, TILE):
            term = lax.dot_general(
                left, turned[k * chunk : (k + 1) * chunk, n : n + TILE], NN,
                preferred_element_type=f32,
            ).reshape(members, columns, TILE)
            if k:
                term = term + acc[:, :columns, n : n + TILE]
            acc[:, :columns, n : n + TILE] = term
    partial(0, 1).start()
    swap.wait()
    for b in range(members):
        for k in range(share):
            opening(beyond, b, k).wait_send()

            @pl.when(jnp.logical_not(home))
            def _():
                opening(r, b, k).wait_send()
    held = jnp.concatenate([state[h] for h in range(nc)], axis=1)
    cube = held * held * held / 3.0
    partial(0, 1).wait()
    place(acc[c, :columns] + part_recv[0] - cube, 0, 1)
    send(1, 2)
    project(LANES)
    sums(0).start()

    def keep(t, rows):
        at = pl.multiple_of(t * columns, columns)
        lanes = lax.broadcasted_iota(jnp.int32, (columns, width), 1)
        sub = lax.broadcasted_iota(jnp.int32, (columns, width), 0) + at
        on = jnp.logical_and(lanes == sub, lanes >= columns)
        aug[pl.ds(at, columns), :] = rows + jnp.where(on, SHIFT, 0.0)

    def gather_sums(slot):
        sums(slot).wait()
        total = sums_send[...] + sums_recv[slot]
        lanes = lax.broadcasted_iota(jnp.int32, (columns, width), 1)
        return total, jnp.where(lanes >= columns, total, 0.0)

    def turn(parts, after, height, t, carry):
        slot, before = lax.rem(t, 2), lax.rem(t + 1, 2)
        for k in range(CHUNKS):
            @pl.when(jnp.logical_not(home))
            def _():
                for b in range(members):
                    arrived(slot, b, k, parts).wait_recv()

            if k == 0:
                @pl.when(home)
                def _():
                    whole(slot, other, parts).wait_recv()

            left = gathered[slot, :, k, : parts * columns].reshape(members * parts * columns, chunk)
            for n in range(0, cells, TILE):
                term = lax.dot_general(
                    left, turned[k * chunk : (k + 1) * chunk, n : n + TILE], NN,
                    preferred_element_type=f32,
                ).reshape(members, parts * columns, TILE)
                if k:
                    term = term + acc[:, : parts * columns, n : n + TILE]
                acc[:, : parts * columns, n : n + TILE] = term
        weighed = weigh(parts)
        if parts == 2:
            part_send[...] = weighed(other)
        partial(slot, parts).start()
        total, projection = gather_sums(before)
        coefficients = split(projection[:, :height])
        gram = total[:, :columns] - product(coefficients, coefficients, NT)
        inverse, lower = factor(gram, (t * columns, width))
        keep(t - 1, projection + lower)
        inverse = split(inverse)
        shift[...] = product(coefficients, (zh[:height], zl[:height]), NN) + SHIFT * cur[before]
        partial(slot, parts).wait_recv()
        image = weighed(c) + part_recv[slot] - shift[...]
        pair = place(product(inverse, split(image), NN), slot, before)
        if after:
            send(before, after)
        here = pl.multiple_of(t * columns, columns)
        zh[pl.ds(here, columns), :], zl[pl.ds(here, columns), :] = pair
        reduced = cur[before] - product(coefficients, (vh[:height], vl[:height]), NN)
        new = split(product(inverse, split(reduced), NN))
        vh[pl.ds(here, columns), :], vl[pl.ds(here, columns), :] = new
        project(height)
        sums(slot).start()
        partial(slot, parts).wait_send()
        for k in range(CHUNKS):
            block(slot, k, parts).wait_send()

        @pl.when(jnp.logical_not(home))
        def _():
            whole(slot, c, parts).wait_send()

        return carry

    first_turn = 1
    while first_turn <= BLOCKS:
        height = -(-(first_turn + 1) * columns // STEP) * STEP
        parts = 2 if first_turn <= WIDE else 1
        after = 0 if first_turn == BLOCKS else 2 if first_turn < WIDE else 1
        last_turn = first_turn
        if first_turn not in (WIDE, BLOCKS):
            last_turn = min(height // columns - 1, BLOCKS - 1)
            if first_turn < WIDE:
                last_turn = min(last_turn, WIDE - 1)
        body = functools.partial(turn, parts, after, height)
        if first_turn == last_turn:
            body(first_turn, 0)
        else:
            lax.fori_loop(first_turn, last_turn + 1, body, 0)
        first_turn = last_turn + 1

    _, projection = gather_sums(BLOCKS % 2)
    keep(BLOCKS, projection)
    load_steps.wait()
    x = aug[...] * (steps_ref[c, 0] / 2.0**SQUARINGS)
    xs = split(x)
    x2 = product(xs, xs, NN)
    x2s = split(x2)
    x3 = product(xs, x2s, NN)
    x4 = product(x2s, x2s, NN)
    tail = x / 120.0 + x2 / 720.0 + x3 / 5040.0 + x4 / 40320.0
    aug[...] = x + x2 / 2.0 + x3 / 6.0 + x4 / 24.0 + product(split(x4), split(tail), NN)

    def square(index, carry):
        now = aug[...]
        pair = split(now)
        aug[...] = 2.0 * now + product(pair, pair, NN)
        return carry

    lax.fori_loop(0, SQUARINGS - 1, square, 0)
    now = aug[...]
    top = now[:columns]
    phi = split(2.0 * top + product(split(top), split(now), NN))
    swap_out = remote(result.at[other], result_recv, o_send, o_recv, r, other)

    def advance(h):
        at = pl.ds(pl.multiple_of(h * length, length), length)
        result[h] = product(phi, (vh[:, at], vl[:, at]), NN)

    advance(other)
    swap_out.start()
    advance(c)
    out_ref[c] = states_ref[c] + result[c]
    swap_out.wait()
    out_ref[other] = states_ref[other] + result_recv[...]


def local(nr, nc, states, jacobian, step_sizes):
    members, columns, length = states.shape
    assert nr == nc == members == 2
    cells = nc * length
    chunk = cells // CHUNKS
    width = -(-(BLOCKS + 1) * columns // LANES) * LANES
    vmem = pl.BlockSpec(memory_space=pltpu.VMEM)
    dma = pltpu.SemaphoreType.DMA
    return pl.pallas_call(
        functools.partial(kernel, nr, nc),
        out_shape=jax.ShapeDtypeStruct(states.shape, f32),
        in_specs=[pl.BlockSpec(memory_space=pl.ANY)] * 3,
        out_specs=vmem,
        scratch_shapes=[
            pltpu.VMEM(states.shape, f32),
            pltpu.SMEM(step_sizes.shape, f32),
            pltpu.VMEM(jacobian.shape, bf16),
            pltpu.VMEM(jacobian.shape[::-1], bf16),
            pltpu.VMEM((members, CHUNKS // nc, columns, chunk), bf16),
            pltpu.VMEM((2, CHUNKS, 2 * columns, chunk), bf16),
            pltpu.VMEM((2, members, CHUNKS, 2 * columns, chunk), bf16),
            pltpu.VMEM((members, 2 * columns, cells), f32),
            pltpu.VMEM((columns, cells), f32),
            pltpu.VMEM((2, columns, cells), f32),
            pltpu.VMEM((width, cells), bf16),
            pltpu.VMEM((width, cells), bf16),
            pltpu.VMEM((width, cells), bf16),
            pltpu.VMEM((width, cells), bf16),
            pltpu.VMEM((2, columns, cells), f32),
            pltpu.VMEM((columns, cells), f32),
            pltpu.VMEM((nc, columns, length), f32),
            pltpu.VMEM((nc, columns, length), f32),
            pltpu.VMEM((columns, length), f32),
            pltpu.VMEM((columns, width), f32),
            pltpu.VMEM((2, columns, width), f32),
            pltpu.VMEM((width, width), f32),
            dma((2,)), dma((LOADS,)), dma((nr, members, CHUNKS)), dma((2, members, CHUNKS)), dma((2, CHUNKS)), dma((2,)), dma((2,)), dma, dma((2,)),
            dma, dma((2,)), dma, dma, dma, dma,
        ],
        compiler_params=pltpu.CompilerParams(
            collective_id=0, has_side_effects=True, vmem_limit_bytes=48 * 2**20
        ),
    )(states, jacobian, step_sizes)


def solution(mesh):
    placed = (P("ens", None, ("row", "col")), P(("ens", "row"), "col"), P("ens", None))
    return jax.shard_map(
        functools.partial(local, mesh.shape["row"], mesh.shape["col"]), mesh=mesh,
        in_specs=placed, out_specs=P("ens", None, ("row", "col")), check_vma=False,
    )
```

```python
import functools

import jax
import jax.numpy as jnp
from jax import lax
from jax.experimental import pallas as pl
from jax.experimental.pallas import tpu as pltpu
from jax.sharding import PartitionSpec as P

BLOCKS = 12
WIDE = 1
SHIFT = -20.5
STEP = 128
SQUARINGS = 10
CHUNKS = 16
TILE = 1024
SIDE = 256
LOADS = 8
GROUP = 16
LANES = 128
MESH = pl.DeviceIdType.MESH
NN = (((1,), (0,)), ((), ()))
NT = (((1,), (1,)), ((), ()))
f32, bf16 = jnp.float32, jnp.bfloat16


def split(value):
    high = value.astype(bf16)
    return high, (value - high.astype(f32)).astype(bf16)


def product(left, right, dims):
    rows = left[0].shape[0]
    both = jnp.concatenate(left, axis=0)
    wide = lax.dot_general(both, right[0], dims, preferred_element_type=f32)
    low = lax.dot_general(left[0], right[1], dims, preferred_element_type=f32)
    return wide[:rows] + (wide[rows:] + low)


def factor(gram, offset):
    columns = gram.shape[0]
    lanes_inv = lax.broadcasted_iota(jnp.int32, (columns, columns), 1)
    sub_inv = lax.broadcasted_iota(jnp.int32, (columns, columns), 0)
    inverse = jnp.where(lanes_inv == sub_inv, 1.0, 0.0).astype(f32)
    lanes = lax.broadcasted_iota(jnp.int32, (columns, offset[1]), 1)
    lower = jnp.zeros((columns, offset[1]), f32)
    sub = lax.broadcasted_iota(jnp.int32, (columns, LANES), 0)
    for base in range(0, columns, GROUP):
        held = [
            jnp.broadcast_to(gram[:, base + i : base + i + 1], (columns, LANES))
            for i in range(GROUP)
        ]
        for i in range(GROUP):
            k = base + i
            pivot = held[i][k : k + 1, :]
            root = lax.rsqrt(pivot)
            root = root * (1.5 - 0.5 * pivot * root * root)
            column = jnp.where(sub >= k, held[i] * root, 0.0)
            below = jnp.where(sub > k, column, 0.0)
            for later in range(i + 1, GROUP):
                index = base + later
                held[later] = held[later] - below * column[index : index + 1, :]
            wide = jnp.concatenate([column] * (offset[1] // LANES), axis=1)
            lower = jnp.where(lanes == offset[0] + k, wide, lower)
            row = gram[k : k + 1, :] * root[:, :columns]
            row_inv = inverse[k : k + 1, :] * root[:, :columns]
            gram = gram - below[:, :columns] * row
            inverse = jnp.where(sub_inv == k, row_inv, inverse - below[:, :columns] * row_inv)
    return inverse, lower


def kernel(
    nr, nc, states_hbm, jac_hbm, steps_hbm, out_ref, states_ref, steps_ref,
    jac, turned, first, own, gathered, acc, part_send, part_recv, vh, vl, zh, zl, cur, shift, state,
    result, result_recv, sums_send, sums_recv, aug,
    in_sem, jac_sem, g_send, g_recv, b_send, d_send, d_recv, p_send, p_recv, s_send, s_recv, x_send, x_recv, o_send, o_recv,
):
    members, columns, length = states_hbm.shape
    cells = nc * length
    chunk = cells // CHUNKS
    share = CHUNKS // nc
    width = vh.shape[0]
    r, c = lax.axis_index("row"), lax.axis_index("col")
    other, beyond = 1 - c, 1 - r
    me = r * nc + c
    count = nr * nc
    home = c == r

    rows = jac.shape[0] // LOADS
    loads = [
        pltpu.make_async_copy(
            jac_hbm.at[i * rows : (i + 1) * rows], jac.at[i * rows : (i + 1) * rows], jac_sem.at[i]
        )
        for i in range(LOADS)
    ]
    load_states = pltpu.make_async_copy(states_hbm, states_ref, in_sem.at[0])
    load_steps = pltpu.make_async_copy(steps_hbm, steps_ref, in_sem.at[1])
    load_states.start()
    load_steps.start()
    for load in loads:
        load.start()
    barrier = pltpu.get_barrier_semaphore()
    for step in range(1, count):
        peer = lax.rem(me + step, count)
        pl.semaphore_signal(
            barrier, inc=1, device_id={"row": peer // nc, "col": lax.rem(peer, nc)},
            device_id_type=MESH,
        )
    load_states.wait()
    for b in range(members):
        rounded = states_ref[b].astype(bf16)
        for k in range(share):
            first[b, k] = rounded[:, k * chunk : (k + 1) * chunk]
    pl.semaphore_wait(barrier, count - 1)

    def remote(src, dst, send, recv, row, col):
        return pltpu.make_async_remote_copy(
            src_ref=src, dst_ref=dst, send_sem=send, recv_sem=recv,
            device_id={"row": row, "col": col}, device_id_type=MESH,
        )

    def opening(row, b, k):
        at = c * share + k
        return remote(
            first.at[b, k], gathered.at[0, b, at, :columns], g_send.at[row, b, at],
            g_recv.at[0, b, at], row, r,
        )

    def opened(b, at):
        return remote(
            first.at[0, 0], gathered.at[0, b, at, :columns], g_send.at[0, b, at],
            g_recv.at[0, b, at], c, other,
        )

    def block(slot, k, parts):
        at = slice(0, parts * columns)
        return remote(
            own.at[slot, k, at], gathered.at[slot, c, k, at], b_send.at[slot, k],
            g_recv.at[slot, c, k], beyond, r,
        )

    def arrived(slot, b, k, parts):
        at = slice(0, parts * columns)
        return remote(
            own.at[slot, k, at], gathered.at[slot, b, k, at], b_send.at[slot, k],
            g_recv.at[slot, b, k], beyond, r,
        )

    def whole(slot, owner, parts):
        at = slice(0, parts * columns)
        return remote(
            own.at[slot, :, at], gathered.at[slot, owner, :, at], d_send.at[slot],
            d_recv.at[slot], r, other,
        )

    def partial(slot, parts):
        source = part_send if parts == 2 else acc.at[other, :columns]
        return remote(source, part_recv.at[slot], p_send, p_recv.at[slot], r, other)

    def sums(slot):
        return remote(sums_send, sums_recv.at[slot], s_send, s_recv.at[slot], beyond, c)

    swap = remote(states_ref.at[other], state.at[c], x_send, x_recv, r, other)

    for b in range(members):
        for k in range(share):
            opening(beyond, b, k).start()
    for b in range(members):
        for k in range(share):
            @pl.when(jnp.logical_not(home))
            def _():
                opening(r, b, k).start()

            @pl.when(home)
            def _():
                gathered[0, b, c * share + k, :columns] = first[b, k]
    swap.start()
    state[c] = states_ref[c]
    for ref in (vh, vl, zh, zl, aug, sums_send):
        ref[...] = jnp.zeros_like(ref)

    def transpose(i, carry):
        at = pl.ds(pl.multiple_of(i * SIDE, SIDE), SIDE)
        for j in range(0, jac.shape[1], SIDE):
            turned[j : j + SIDE, at] = jac[at, j : j + SIDE].T
        return carry

    for i in range(LOADS):
        loads[i].wait()
        lax.fori_loop(i * (rows // SIDE), (i + 1) * (rows // SIDE), transpose, 0)

    def weigh(parts):
        if parts == 2:
            return lambda b: acc[b, :columns] + acc[b, columns:]
        return lambda b: acc[b, :columns]

    def place(now, slot, out):
        pair = split(now)
        cur[slot] = now
        vh[:columns], vl[:columns] = pair
        both = jnp.concatenate(pair, axis=0)
        for k in range(CHUNKS):
            own[out, k] = both[:, k * chunk : (k + 1) * chunk]
        return pair

    def send(slot, parts):
        for k in range(CHUNKS):
            block(slot, k, parts).start()

        @pl.when(jnp.logical_not(home))
        def _():
            whole(slot, c, parts).start()

        @pl.when(home)
        def _():
            at = slice(0, parts * columns)
            gathered[slot, c, :, at] = own[slot, :, at]

    def project(height):
        at = slice(0, height)
        pair = jnp.concatenate([vh[:columns], vl[:columns]], axis=0)
        wide = lax.dot_general(vh[at], pair, NT, preferred_element_type=f32)
        low = lax.dot_general(vl[at], pair[:columns], NT, preferred_element_type=f32)
        sums_send[:, at] = (wide[:, :columns] + (wide[:, columns:] + low)).T

    for k in range(CHUNKS):
        for b in range(members):
            @pl.when(jnp.logical_not(jnp.logical_and(home, k // share == c)))
            def _():
                opened(b, k).wait_recv()

        left = gathered[0, :, k, :columns].reshape(members * columns, chunk)
        for n in range(0, cells, TILE):
            term = lax.dot_general(
                left, turned[k * chunk : (k + 1) * chunk, n : n + TILE], NN,
                preferred_element_type=f32,
            ).reshape(members, columns, TILE)
            if k:
                term = term + acc[:, :columns, n : n + TILE]
            acc[:, :columns, n : n + TILE] = term
    partial(0, 1).start()
    swap.wait()
    for b in range(members):
        for k in range(share):
            opening(beyond, b, k).wait_send()

            @pl.when(jnp.logical_not(home))
            def _():
                opening(r, b, k).wait_send()
    held = jnp.concatenate([state[h] for h in range(nc)], axis=1)
    cube = held * held * held / 3.0
    partial(0, 1).wait()
    place(acc[c, :columns] + part_recv[0] - cube, 0, 1)
    send(1, 2)
    project(LANES)
    sums(0).start()

    def keep(t, rows):
        at = pl.multiple_of(t * columns, columns)
        lanes = lax.broadcasted_iota(jnp.int32, (columns, width), 1)
        sub = lax.broadcasted_iota(jnp.int32, (columns, width), 0) + at
        on = jnp.logical_and(lanes == sub, lanes >= columns)
        aug[pl.ds(at, columns), :] = rows + jnp.where(on, SHIFT, 0.0)

    def gather_sums(slot):
        sums(slot).wait()
        total = sums_send[...] + sums_recv[slot]
        lanes = lax.broadcasted_iota(jnp.int32, (columns, width), 1)
        return total, jnp.where(lanes >= columns, total, 0.0)

    def turn(parts, after, height, t, carry):
        slot, before = lax.rem(t, 2), lax.rem(t + 1, 2)
        for k in range(CHUNKS):
            @pl.when(jnp.logical_not(home))
            def _():
                for b in range(members):
                    arrived(slot, b, k, parts).wait_recv()

            if k == 0:
                @pl.when(home)
                def _():
                    whole(slot, other, parts).wait_recv()

            left = gathered[slot, :, k, : parts * columns].reshape(members * parts * columns, chunk)
            for n in range(0, cells, TILE):
                term = lax.dot_general(
                    left, turned[k * chunk : (k + 1) * chunk, n : n + TILE], NN,
                    preferred_element_type=f32,
                ).reshape(members, parts * columns, TILE)
                if k:
                    term = term + acc[:, : parts * columns, n : n + TILE]
                acc[:, : parts * columns, n : n + TILE] = term
        weighed = weigh(parts)
        if parts == 2:
            part_send[...] = weighed(other)
        partial(slot, parts).start()
        total, projection = gather_sums(before)
        coefficients = split(projection[:, :height])
        gram = total[:, :columns] - product(coefficients, coefficients, NT)
        inverse, lower = factor(gram, (t * columns, width))
        keep(t - 1, projection + lower)
        inverse = split(inverse)
        shift[...] = product(coefficients, (zh[:height], zl[:height]), NN) + SHIFT * cur[before]
        partial(slot, parts).wait_recv()
        image = weighed(c) + part_recv[slot] - shift[...]
        pair = place(product(inverse, split(image), NN), slot, before)
        if after:
            send(before, after)
        here = pl.multiple_of(t * columns, columns)
        zh[pl.ds(here, columns), :], zl[pl.ds(here, columns), :] = pair
        reduced = cur[before] - product(coefficients, (vh[:height], vl[:height]), NN)
        new = split(product(inverse, split(reduced), NN))
        vh[pl.ds(here, columns), :], vl[pl.ds(here, columns), :] = new
        project(height)
        sums(slot).start()
        partial(slot, parts).wait_send()
        for k in range(CHUNKS):
            block(slot, k, parts).wait_send()

        @pl.when(jnp.logical_not(home))
        def _():
            whole(slot, c, parts).wait_send()

        return carry

    first_turn = 1
    while first_turn <= BLOCKS:
        height = -(-(first_turn + 1) * columns // STEP) * STEP
        parts = 2 if first_turn <= WIDE else 1
        after = 0 if first_turn == BLOCKS else 2 if first_turn < WIDE else 1
        last_turn = first_turn
        if first_turn not in (WIDE, BLOCKS):
            last_turn = min(height // columns - 1, BLOCKS - 1)
            if first_turn < WIDE:
                last_turn = min(last_turn, WIDE - 1)
        body = functools.partial(turn, parts, after, height)
        if first_turn == last_turn:
            body(first_turn, 0)
        else:
            lax.fori_loop(first_turn, last_turn + 1, body, 0)
        first_turn = last_turn + 1

    _, projection = gather_sums(BLOCKS % 2)
    keep(BLOCKS, projection)
    load_steps.wait()
    x = aug[...] * (steps_ref[c, 0] / 2.0**SQUARINGS)
    xs = split(x)
    x2 = product(xs, xs, NN)
    x2s = split(x2)
    x3 = product(xs, x2s, NN)
    x4 = product(x2s, x2s, NN)
    tail = x / 120.0 + x2 / 720.0 + x3 / 5040.0 + x4 / 40320.0
    aug[...] = x + x2 / 2.0 + x3 / 6.0 + x4 / 24.0 + product(split(x4), split(tail), NN)

    used = (BLOCKS + 1) * columns

    def square(index, carry):
        high, low = split(aug[...])
        aug[:used] = 2.0 * aug[:used] + product((high[:used], low[:used]), (high, low), NN)
        return carry

    lax.fori_loop(0, SQUARINGS - 1, square, 0)
    now = aug[...]
    top = now[:columns]
    phi = split(2.0 * top + product(split(top), split(now), NN))
    swap_out = remote(result.at[other], result_recv, o_send, o_recv, r, other)

    def advance(h):
        at = pl.ds(pl.multiple_of(h * length, length), length)
        result[h] = product(phi, (vh[:, at], vl[:, at]), NN)

    advance(other)
    swap_out.start()
    advance(c)
    out_ref[c] = states_ref[c] + result[c]
    swap_out.wait()
    out_ref[other] = states_ref[other] + result_recv[...]


def local(nr, nc, states, jacobian, step_sizes):
    members, columns, length = states.shape
    assert nr == nc == members == 2
    cells = nc * length
    chunk = cells // CHUNKS
    width = -(-(BLOCKS + 1) * columns // LANES) * LANES
    vmem = pl.BlockSpec(memory_space=pltpu.VMEM)
    dma = pltpu.SemaphoreType.DMA
    return pl.pallas_call(
        functools.partial(kernel, nr, nc),
        out_shape=jax.ShapeDtypeStruct(states.shape, f32),
        in_specs=[pl.BlockSpec(memory_space=pl.ANY)] * 3,
        out_specs=vmem,
        scratch_shapes=[
            pltpu.VMEM(states.shape, f32),
            pltpu.SMEM(step_sizes.shape, f32),
            pltpu.VMEM(jacobian.shape, bf16),
            pltpu.VMEM(jacobian.shape[::-1], bf16),
            pltpu.VMEM((members, CHUNKS // nc, columns, chunk), bf16),
            pltpu.VMEM((2, CHUNKS, 2 * columns, chunk), bf16),
            pltpu.VMEM((2, members, CHUNKS, 2 * columns, chunk), bf16),
            pltpu.VMEM((members, 2 * columns, cells), f32),
            pltpu.VMEM((columns, cells), f32),
            pltpu.VMEM((2, columns, cells), f32),
            pltpu.VMEM((width, cells), bf16),
            pltpu.VMEM((width, cells), bf16),
            pltpu.VMEM((width, cells), bf16),
            pltpu.VMEM((width, cells), bf16),
            pltpu.VMEM((2, columns, cells), f32),
            pltpu.VMEM((columns, cells), f32),
            pltpu.VMEM((nc, columns, length), f32),
            pltpu.VMEM((nc, columns, length), f32),
            pltpu.VMEM((columns, length), f32),
            pltpu.VMEM((columns, width), f32),
            pltpu.VMEM((2, columns, width), f32),
            pltpu.VMEM((width, width), f32),
            dma((2,)), dma((LOADS,)), dma((nr, members, CHUNKS)), dma((2, members, CHUNKS)), dma((2, CHUNKS)), dma((2,)), dma((2,)), dma, dma((2,)),
            dma, dma((2,)), dma, dma, dma, dma,
        ],
        compiler_params=pltpu.CompilerParams(
            collective_id=0, has_side_effects=True, vmem_limit_bytes=48 * 2**20
        ),
    )(states, jacobian, step_sizes)


def solution(mesh):
    placed = (P("ens", None, ("row", "col")), P(("ens", "row"), "col"), P("ens", None))
    return jax.shard_map(
        functools.partial(local, mesh.shape["row"], mesh.shape["col"]), mesh=mesh,
        in_specs=placed, out_specs=P("ens", None, ("row", "col")), check_vma=False,
    )
```

```python
import functools

import jax
import jax.numpy as jnp
from jax import lax
from jax.experimental import pallas as pl
from jax.experimental.pallas import tpu as pltpu
from jax.sharding import PartitionSpec as P

BLOCKS = 12
WIDE = 1
SHIFT = -20.5
STEP = 128
SQUARINGS = 10
CHUNKS = 16
TILE = 2048
SIDE = 256
LOADS = 8
GROUP = 16
LANES = 128
MESH = pl.DeviceIdType.MESH
NN = (((1,), (0,)), ((), ()))
NT = (((1,), (1,)), ((), ()))
f32, bf16 = jnp.float32, jnp.bfloat16


def split(value):
    high = value.astype(bf16)
    return high, (value - high.astype(f32)).astype(bf16)


def product(left, right, dims):
    rows = left[0].shape[0]
    both = jnp.concatenate(left, axis=0)
    wide = lax.dot_general(both, right[0], dims, preferred_element_type=f32)
    low = lax.dot_general(left[0], right[1], dims, preferred_element_type=f32)
    return wide[:rows] + (wide[rows:] + low)


def factor(gram, offset):
    columns = gram.shape[0]
    lanes_inv = lax.broadcasted_iota(jnp.int32, (columns, columns), 1)
    sub_inv = lax.broadcasted_iota(jnp.int32, (columns, columns), 0)
    inverse = jnp.where(lanes_inv == sub_inv, 1.0, 0.0).astype(f32)
    lanes = lax.broadcasted_iota(jnp.int32, (columns, offset[1]), 1)
    lower = jnp.zeros((columns, offset[1]), f32)
    sub = lax.broadcasted_iota(jnp.int32, (columns, LANES), 0)
    for base in range(0, columns, GROUP):
        held = [
            jnp.broadcast_to(gram[:, base + i : base + i + 1], (columns, LANES))
            for i in range(GROUP)
        ]
        for i in range(GROUP):
            k = base + i
            pivot = held[i][k : k + 1, :]
            root = lax.rsqrt(pivot)
            root = root * (1.5 - 0.5 * pivot * root * root)
            column = jnp.where(sub >= k, held[i] * root, 0.0)
            below = jnp.where(sub > k, column, 0.0)
            for later in range(i + 1, GROUP):
                index = base + later
                held[later] = held[later] - below * column[index : index + 1, :]
            wide = jnp.concatenate([column] * (offset[1] // LANES), axis=1)
            lower = jnp.where(lanes == offset[0] + k, wide, lower)
            row = gram[k : k + 1, :] * root[:, :columns]
            row_inv = inverse[k : k + 1, :] * root[:, :columns]
            gram = gram - below[:, :columns] * row
            inverse = jnp.where(sub_inv == k, row_inv, inverse - below[:, :columns] * row_inv)
    return inverse, lower


def kernel(
    nr, nc, states_hbm, jac_hbm, steps_hbm, out_ref, states_ref, steps_ref,
    jac, turned, first, own, gathered, acc, part_send, part_recv, vh, vl, zh, zl, cur, shift, state,
    result, result_recv, sums_send, sums_recv, aug,
    in_sem, jac_sem, g_send, g_recv, b_send, d_send, d_recv, p_send, p_recv, s_send, s_recv, x_send, x_recv, o_send, o_recv,
):
    members, columns, length = states_hbm.shape
    cells = nc * length
    chunk = cells // CHUNKS
    share = CHUNKS // nc
    width = vh.shape[0]
    r, c = lax.axis_index("row"), lax.axis_index("col")
    other, beyond = 1 - c, 1 - r
    me = r * nc + c
    count = nr * nc
    home = c == r

    rows = jac.shape[0] // LOADS
    loads = [
        pltpu.make_async_copy(
            jac_hbm.at[i * rows : (i + 1) * rows], jac.at[i * rows : (i + 1) * rows], jac_sem.at[i]
        )
        for i in range(LOADS)
    ]
    load_states = pltpu.make_async_copy(states_hbm, states_ref, in_sem.at[0])
    load_steps = pltpu.make_async_copy(steps_hbm, steps_ref, in_sem.at[1])
    load_states.start()
    load_steps.start()
    for load in loads:
        load.start()
    barrier = pltpu.get_barrier_semaphore()
    for step in range(1, count):
        peer = lax.rem(me + step, count)
        pl.semaphore_signal(
            barrier, inc=1, device_id={"row": peer // nc, "col": lax.rem(peer, nc)},
            device_id_type=MESH,
        )
    load_states.wait()
    for b in range(members):
        rounded = states_ref[b].astype(bf16)
        for k in range(share):
            first[b, k] = rounded[:, k * chunk : (k + 1) * chunk]
    pl.semaphore_wait(barrier, count - 1)

    def remote(src, dst, send, recv, row, col):
        return pltpu.make_async_remote_copy(
            src_ref=src, dst_ref=dst, send_sem=send, recv_sem=recv,
            device_id={"row": row, "col": col}, device_id_type=MESH,
        )

    def opening(row, b, k):
        at = c * share + k
        return remote(
            first.at[b, k], gathered.at[0, b, at, :columns], g_send.at[row, b, at],
            g_recv.at[0, b, at], row, r,
        )

    def opened(b, at):
        return remote(
            first.at[0, 0], gathered.at[0, b, at, :columns], g_send.at[0, b, at],
            g_recv.at[0, b, at], c, other,
        )

    def block(slot, k, parts):
        at = slice(0, parts * columns)
        return remote(
            own.at[slot, k, at], gathered.at[slot, c, k, at], b_send.at[slot, k],
            g_recv.at[slot, c, k], beyond, r,
        )

    def arrived(slot, b, k, parts):
        at = slice(0, parts * columns)
        return remote(
            own.at[slot, k, at], gathered.at[slot, b, k, at], b_send.at[slot, k],
            g_recv.at[slot, b, k], beyond, r,
        )

    def whole(slot, owner, parts):
        at = slice(0, parts * columns)
        return remote(
            own.at[slot, :, at], gathered.at[slot, owner, :, at], d_send.at[slot],
            d_recv.at[slot], r, other,
        )

    def partial(slot, parts):
        source = part_send if parts == 2 else acc.at[other, :columns]
        return remote(source, part_recv.at[slot], p_send, p_recv.at[slot], r, other)

    def sums(slot):
        return remote(sums_send, sums_recv.at[slot], s_send, s_recv.at[slot], beyond, c)

    swap = remote(states_ref.at[other], state.at[c], x_send, x_recv, r, other)

    for b in range(members):
        for k in range(share):
            opening(beyond, b, k).start()
    for b in range(members):
        for k in range(share):
            @pl.when(jnp.logical_not(home))
            def _():
                opening(r, b, k).start()

            @pl.when(home)
            def _():
                gathered[0, b, c * share + k, :columns] = first[b, k]
    swap.start()
    state[c] = states_ref[c]
    for ref in (vh, vl, zh, zl, aug, sums_send):
        ref[...] = jnp.zeros_like(ref)

    def transpose(i, carry):
        at = pl.ds(pl.multiple_of(i * SIDE, SIDE), SIDE)
        for j in range(0, jac.shape[1], SIDE):
            turned[j : j + SIDE, at] = jac[at, j : j + SIDE].T
        return carry

    for i in range(LOADS):
        loads[i].wait()
        lax.fori_loop(i * (rows // SIDE), (i + 1) * (rows // SIDE), transpose, 0)

    def weigh(parts):
        if parts == 2:
            return lambda b: acc[b, :columns] + acc[b, columns:]
        return lambda b: acc[b, :columns]

    def place(now, slot, out):
        pair = split(now)
        cur[slot] = now
        vh[:columns], vl[:columns] = pair
        both = jnp.concatenate(pair, axis=0)
        for k in range(CHUNKS):
            own[out, k] = both[:, k * chunk : (k + 1) * chunk]
        return pair

    def send(slot, parts):
        for k in range(CHUNKS):
            block(slot, k, parts).start()

        @pl.when(jnp.logical_not(home))
        def _():
            whole(slot, c, parts).start()

        @pl.when(home)
        def _():
            at = slice(0, parts * columns)
            gathered[slot, c, :, at] = own[slot, :, at]

    def project(height):
        at = slice(0, height)
        pair = jnp.concatenate([vh[:columns], vl[:columns]], axis=0)
        wide = lax.dot_general(vh[at], pair, NT, preferred_element_type=f32)
        low = lax.dot_general(vl[at], pair[:columns], NT, preferred_element_type=f32)
        sums_send[:, at] = (wide[:, :columns] + (wide[:, columns:] + low)).T

    for k in range(CHUNKS):
        for b in range(members):
            @pl.when(jnp.logical_not(jnp.logical_and(home, k // share == c)))
            def _():
                opened(b, k).wait_recv()

        left = gathered[0, :, k, :columns].reshape(members * columns, chunk)
        for n in range(0, cells, TILE):
            term = lax.dot_general(
                left, turned[k * chunk : (k + 1) * chunk, n : n + TILE], NN,
                preferred_element_type=f32,
            ).reshape(members, columns, TILE)
            if k:
                term = term + acc[:, :columns, n : n + TILE]
            acc[:, :columns, n : n + TILE] = term
    partial(0, 1).start()
    swap.wait()
    for b in range(members):
        for k in range(share):
            opening(beyond, b, k).wait_send()

            @pl.when(jnp.logical_not(home))
            def _():
                opening(r, b, k).wait_send()
    held = jnp.concatenate([state[h] for h in range(nc)], axis=1)
    cube = held * held * held / 3.0
    partial(0, 1).wait()
    place(acc[c, :columns] + part_recv[0] - cube, 0, 1)
    send(1, 2)
    project(LANES)
    sums(0).start()

    def keep(t, rows):
        at = pl.multiple_of(t * columns, columns)
        lanes = lax.broadcasted_iota(jnp.int32, (columns, width), 1)
        sub = lax.broadcasted_iota(jnp.int32, (columns, width), 0) + at
        on = jnp.logical_and(lanes == sub, lanes >= columns)
        aug[pl.ds(at, columns), :] = rows + jnp.where(on, SHIFT, 0.0)

    def gather_sums(slot):
        sums(slot).wait()
        total = sums_send[...] + sums_recv[slot]
        lanes = lax.broadcasted_iota(jnp.int32, (columns, width), 1)
        return total, jnp.where(lanes >= columns, total, 0.0)

    def turn(parts, after, height, t, carry):
        slot, before = lax.rem(t, 2), lax.rem(t + 1, 2)
        for k in range(CHUNKS):
            @pl.when(jnp.logical_not(home))
            def _():
                for b in range(members):
                    arrived(slot, b, k, parts).wait_recv()

            if k == 0:
                @pl.when(home)
                def _():
                    whole(slot, other, parts).wait_recv()

            left = gathered[slot, :, k, : parts * columns].reshape(members * parts * columns, chunk)
            for n in range(0, cells, TILE):
                term = lax.dot_general(
                    left, turned[k * chunk : (k + 1) * chunk, n : n + TILE], NN,
                    preferred_element_type=f32,
                ).reshape(members, parts * columns, TILE)
                if k:
                    term = term + acc[:, : parts * columns, n : n + TILE]
                acc[:, : parts * columns, n : n + TILE] = term
        weighed = weigh(parts)
        if parts == 2:
            part_send[...] = weighed(other)
        partial(slot, parts).start()
        total, projection = gather_sums(before)
        coefficients = split(projection[:, :height])
        gram = total[:, :columns] - product(coefficients, coefficients, NT)
        inverse, lower = factor(gram, (t * columns, width))
        keep(t - 1, projection + lower)
        inverse = split(inverse)
        shift[...] = product(coefficients, (zh[:height], zl[:height]), NN) + SHIFT * cur[before]
        partial(slot, parts).wait_recv()
        image = weighed(c) + part_recv[slot] - shift[...]
        pair = place(product(inverse, split(image), NN), slot, before)
        if after:
            send(before, after)
        here = pl.multiple_of(t * columns, columns)
        zh[pl.ds(here, columns), :], zl[pl.ds(here, columns), :] = pair
        reduced = cur[before] - product(coefficients, (vh[:height], vl[:height]), NN)
        new = split(product(inverse, split(reduced), NN))
        vh[pl.ds(here, columns), :], vl[pl.ds(here, columns), :] = new
        project(height)
        sums(slot).start()
        partial(slot, parts).wait_send()
        for k in range(CHUNKS):
            block(slot, k, parts).wait_send()

        @pl.when(jnp.logical_not(home))
        def _():
            whole(slot, c, parts).wait_send()

        return carry

    first_turn = 1
    while first_turn <= BLOCKS:
        height = -(-(first_turn + 1) * columns // STEP) * STEP
        parts = 2 if first_turn <= WIDE else 1
        after = 0 if first_turn == BLOCKS else 2 if first_turn < WIDE else 1
        last_turn = first_turn
        if first_turn not in (WIDE, BLOCKS):
            last_turn = min(height // columns - 1, BLOCKS - 1)
            if first_turn < WIDE:
                last_turn = min(last_turn, WIDE - 1)
        body = functools.partial(turn, parts, after, height)
        if first_turn == last_turn:
            body(first_turn, 0)
        else:
            lax.fori_loop(first_turn, last_turn + 1, body, 0)
        first_turn = last_turn + 1

    _, projection = gather_sums(BLOCKS % 2)
    keep(BLOCKS, projection)
    load_steps.wait()
    x = aug[...] * (steps_ref[c, 0] / 2.0**SQUARINGS)
    xs = split(x)
    x2 = product(xs, xs, NN)
    x2s = split(x2)
    x3 = product(xs, x2s, NN)
    x4 = product(x2s, x2s, NN)
    tail = x / 120.0 + x2 / 720.0 + x3 / 5040.0 + x4 / 40320.0
    aug[...] = x + x2 / 2.0 + x3 / 6.0 + x4 / 24.0 + product(split(x4), split(tail), NN)

    used = (BLOCKS + 1) * columns

    def square(index, carry):
        high, low = split(aug[...])
        aug[:used] = 2.0 * aug[:used] + product((high[:used], low[:used]), (high, low), NN)
        return carry

    lax.fori_loop(0, SQUARINGS - 1, square, 0)
    now = aug[...]
    top = now[:columns]
    phi = split(2.0 * top + product(split(top), split(now), NN))
    swap_out = remote(result.at[other], result_recv, o_send, o_recv, r, other)

    def advance(h):
        at = pl.ds(pl.multiple_of(h * length, length), length)
        result[h] = product(phi, (vh[:, at], vl[:, at]), NN)

    advance(other)
    swap_out.start()
    advance(c)
    out_ref[c] = states_ref[c] + result[c]
    swap_out.wait()
    out_ref[other] = states_ref[other] + result_recv[...]


def local(nr, nc, states, jacobian, step_sizes):
    members, columns, length = states.shape
    assert nr == nc == members == 2
    cells = nc * length
    chunk = cells // CHUNKS
    width = -(-(BLOCKS + 1) * columns // LANES) * LANES
    vmem = pl.BlockSpec(memory_space=pltpu.VMEM)
    dma = pltpu.SemaphoreType.DMA
    return pl.pallas_call(
        functools.partial(kernel, nr, nc),
        out_shape=jax.ShapeDtypeStruct(states.shape, f32),
        in_specs=[pl.BlockSpec(memory_space=pl.ANY)] * 3,
        out_specs=vmem,
        scratch_shapes=[
            pltpu.VMEM(states.shape, f32),
            pltpu.SMEM(step_sizes.shape, f32),
            pltpu.VMEM(jacobian.shape, bf16),
            pltpu.VMEM(jacobian.shape[::-1], bf16),
            pltpu.VMEM((members, CHUNKS // nc, columns, chunk), bf16),
            pltpu.VMEM((2, CHUNKS, 2 * columns, chunk), bf16),
            pltpu.VMEM((2, members, CHUNKS, 2 * columns, chunk), bf16),
            pltpu.VMEM((members, 2 * columns, cells), f32),
            pltpu.VMEM((columns, cells), f32),
            pltpu.VMEM((2, columns, cells), f32),
            pltpu.VMEM((width, cells), bf16),
            pltpu.VMEM((width, cells), bf16),
            pltpu.VMEM((width, cells), bf16),
            pltpu.VMEM((width, cells), bf16),
            pltpu.VMEM((2, columns, cells), f32),
            pltpu.VMEM((columns, cells), f32),
            pltpu.VMEM((nc, columns, length), f32),
            pltpu.VMEM((nc, columns, length), f32),
            pltpu.VMEM((columns, length), f32),
            pltpu.VMEM((columns, width), f32),
            pltpu.VMEM((2, columns, width), f32),
            pltpu.VMEM((width, width), f32),
            dma((2,)), dma((LOADS,)), dma((nr, members, CHUNKS)), dma((2, members, CHUNKS)), dma((2, CHUNKS)), dma((2,)), dma((2,)), dma, dma((2,)),
            dma, dma((2,)), dma, dma, dma, dma,
        ],
        compiler_params=pltpu.CompilerParams(
            collective_id=0, has_side_effects=True, vmem_limit_bytes=48 * 2**20
        ),
    )(states, jacobian, step_sizes)


def solution(mesh):
    placed = (P("ens", None, ("row", "col")), P(("ens", "row"), "col"), P("ens", None))
    return jax.shard_map(
        functools.partial(local, mesh.shape["row"], mesh.shape["col"]), mesh=mesh,
        in_specs=placed, out_specs=P("ens", None, ("row", "col")), check_vma=False,
    )
```
